128 devices in a mesh: row: 8 (over z_hi, y), col: 16 (over z_lo, x, core).
Axes of the slice: x: 4, y: 4, z: 4 (z_hi: 2, z_lo: 2; z = z_hi * 2 + z_lo), core: 2. Of those that a mesh axis runs over, the one named last changes fastest.
Arguments:
- features: bfloat16 [65536, 256], P(('col', 'row')), may hold values from -6 to 6
- weight: bfloat16 [256, 256], replicated, may hold values from -0.375 to 0.375
- bias: float32 [256], replicated, may hold values from -4 to 4
- cotangent: bfloat16 [65536, 256], P(('row', 'col')), may hold values from -6 to 6
- tiles: bfloat16 [8, 16, 384, 128, 128], P('row', 'col'), may hold values from -0.0546875 to 0.0546875
- tile_rows: int32 [8, 16, 384], P('row', 'col'), may hold values from 0 to 63, as said below
- tile_cols: int32 [8, 16, 384], P('row', 'col'), may hold values from 0 to 31
- tile_counts: int32 [8, 16], P('row', 'col'), may hold values from 24 to 384, as said below
Outputs:
- hidden: bfloat16 [65536, 256], P(('row', 'col'))
- grad_weight: float32 [256, 256], replicated
- grad_bias: float32 [256], replicated
- grad_features: bfloat16 [65536, 256], P(('col', 'row'))
The draws below stay inside these ranges and needn't reach their ends.
Inputs may be any that keep to these rules, and one draw needn't show every extreme that they name: `tile_rows`: on each grid cell the slots name distinct blocks. `tile_counts`: slots at or after a cell's count are unused; some cell uses all 384 slots.
All inputs are finite; a program needn't handle non-finite values.
Results may differ from the reference program's by a relative error of at most 0.013.
Values may be sent and summed in bfloat16 or wider, within the bound.
A program may use at most 128 MiB of HBM per device.

```python
import math
import jax
import jax.numpy as jnp
from jax import lax

F = 256
BLOCK = 128
NODE_DEV = 512
TILES_CAP = 384
NODES = 65536
BLK_ROWS = 64
BLK_COLS = 32
N_ROW = 8
N_COL = 16


def tile_slots(key):
    cell_keys = jax.random.split(jax.random.fold_in(key, 7), N_ROW * N_COL)

    def one_cell(cell_key):
        return jax.random.permutation(cell_key, BLK_ROWS * BLK_COLS)[:TILES_CAP]
    chosen = jax.vmap(one_cell)(cell_keys)
    return chosen.reshape(N_ROW, N_COL, TILES_CAP).astype(jnp.int32)


def draw_tile_rows(key, part):
    return (tile_slots(key) // BLK_COLS).astype(jnp.int32)


def draw_tile_cols(key, part):
    return (tile_slots(key) % BLK_COLS).astype(jnp.int32)


def draw_tile_counts(key, part):
    first_key = jax.random.fold_in(key, 11)
    second_key = jax.random.fold_in(key, 13)
    third_key = jax.random.fold_in(key, 17)
    first = jax.random.randint(first_key, (N_ROW * N_COL,), 1, 5)
    second = jax.random.randint(second_key, (N_ROW * N_COL,), 1, 5)
    fullest = jax.random.randint(third_key, (), 0, N_ROW * N_COL)
    shares = first * second
    shares = jnp.where(jnp.arange(N_ROW * N_COL) == fullest, 16, shares)
    return (TILES_CAP * shares // 16).reshape(N_ROW, N_COL).astype(jnp.int32)


def levels(own_key, extent, pieces, smallest, top_value):
    def one(dim, blocks):
        heights = jax.random.uniform(jax.random.fold_in(jax.random.fold_in(own_key, 6), dim), (blocks,), jnp.float32, smallest / len(pieces), top_value / len(pieces))
        return jnp.repeat(jnp.exp(heights), extent[dim] // blocks).reshape((-1,) + (1,) * (len(extent) - dim - 1))

    level = one(*pieces[0])
    for cut in pieces[1:]:
        level = level * one(*cut)
    return level


def gaussian(key, dims, spread, reach, cuts=(), kind=jnp.bfloat16):
    drawn = spread * jax.random.normal(key, dims, jnp.float32)
    if cuts:
        drawn = drawn * levels(key, dims, cuts, -0.22, 0.18)
    return jnp.clip(drawn, -reach, reach).astype(kind)


def setup_inputs(seed: int = 0) -> dict:
    key_of = jax.random.split(jax.random.key(seed), 9)
    features = gaussian(key_of[0], (NODES, F), 1.0, 6.0, ((0, 128),))
    weight = gaussian(key_of[1], (F, F), F ** -0.5, 0.375)
    bias = gaussian(key_of[2], (F,), 1.0, 4.0, (), jnp.float32)
    cotangent = gaussian(key_of[3], (NODES, F), 1.0, 6.0, ((0, 128),))
    tiles = gaussian(key_of[4], (N_ROW, N_COL, TILES_CAP, BLOCK, BLOCK), (TILES_CAP * BLOCK * BLOCK // NODE_DEV) ** -0.5, 0.0546875, ((0, 8), (1, 16)))
    tile_rows = draw_tile_rows(jax.random.fold_in(key_of[8], 71), 0)
    tile_cols = draw_tile_cols(jax.random.fold_in(key_of[8], 71), 0)
    tile_counts = draw_tile_counts(jax.random.fold_in(key_of[8], 71), 0)
    return {"features": features, "weight": weight, "bias": bias, "cotangent": cotangent, "tiles": tiles, "tile_rows": tile_rows, "tile_cols": tile_cols, "tile_counts": tile_counts}


def reference(features, weight, bias, cotangent, tiles, tile_rows, tile_cols, tile_counts):
    nodes = features.shape[0]
    feat_blocks = features.reshape(nodes // BLOCK, BLOCK, F)
    cells = jnp.arange(N_ROW * N_COL, dtype=jnp.int32)
    slot_ids = jnp.arange(TILES_CAP, dtype=jnp.int32)

    def cell_parts(index):
        row_pos = index // N_COL
        col_pos = index % N_COL
        tile_set = tiles[row_pos, col_pos].astype(jnp.float32)
        dest = (row_pos * BLK_ROWS + tile_rows[row_pos, col_pos]).astype(jnp.int32)
        source = (col_pos * BLK_COLS + tile_cols[row_pos, col_pos]).astype(jnp.int32)
        live = slot_ids < tile_counts[row_pos, col_pos]
        return (tile_set, dest, source, live)

    def forward_cell(total, index):
        tile_set, dest, source, live = cell_parts(index)
        contrib = jnp.einsum('tij,tjf->tif', tile_set, feat_blocks[source].astype(jnp.float32))
        contrib = jnp.where(live[:, None, None], contrib, jnp.zeros_like(contrib))
        return (total.at[dest].add(contrib), None)
    start_total = jnp.zeros((nodes // BLOCK, BLOCK, F), jnp.float32)
    total, unused = lax_scan(forward_cell, start_total, cells)
    aggregated = total.reshape(nodes, F).astype(jnp.bfloat16)
    preact = jnp.dot(aggregated, weight, preferred_element_type=jnp.float32) + bias.astype(jnp.float32)
    hidden = jax.nn.silu(preact).astype(jnp.bfloat16)
    sigma = jax.nn.sigmoid(preact)
    slope = sigma * (1.0 + preact * (1.0 - sigma))
    grad_pre = (cotangent.astype(jnp.float32) * slope).astype(jnp.bfloat16)
    factor = 1.0 / math.sqrt(nodes)
    grad_weight = jnp.dot(aggregated.T, grad_pre, preferred_element_type=jnp.float32) * factor
    grad_bias = lax.optimization_barrier(jnp.sum(grad_pre.astype(jnp.float32), axis=0)) * factor
    grad_agg = jnp.dot(grad_pre, weight.T, preferred_element_type=jnp.float32).astype(jnp.bfloat16)
    grad_blocks = grad_agg.reshape(nodes // BLOCK, BLOCK, F)

    def backward_cell(total_back, index):
        tile_set, dest, source, live = cell_parts(index)
        contrib = jnp.einsum('tji,tjf->tif', tile_set, grad_blocks[dest].astype(jnp.float32))
        contrib = jnp.where(live[:, None, None], contrib, jnp.zeros_like(contrib))
        return (total_back.at[source].add(contrib), None)
    total_back, unused = lax_scan(backward_cell, jnp.zeros((nodes // BLOCK, BLOCK, F), jnp.float32), cells)
    grad_features = total_back.reshape(nodes, F).astype(jnp.bfloat16)
    return (hidden, grad_weight, grad_bias, grad_features)

def lax_scan(function, carry, values):
    return jax.lax.scan(function, carry, values)
```

```python
import functools
import math

import jax
import jax.numpy as jnp
from jax import lax
from jax.experimental import pallas as pl
from jax.experimental.pallas import tpu as pltpu
from jax.sharding import PartitionSpec as P

GROUP = 32


def accumulate_kernel(backward, dest_ref, source_ref, count_ref, tiles_ref, panel_ref, out_ref):
    step = pl.program_id(0)
    group = tiles_ref.shape[0]
    out_blocks = out_ref.shape[0]
    in_blocks = panel_ref.shape[0]

    @pl.when(step == 0)
    def _():
        out_ref[...] = jnp.zeros_like(out_ref)

    base = step * group
    live_count = count_ref[0]

    def one_tile(i, carry):
        slot = base + i

        @pl.when(slot < live_count)
        def _():
            if backward:
                fetch = jnp.clip(dest_ref[slot], 0, in_blocks - 1)
                target = jnp.clip(source_ref[slot], 0, out_blocks - 1)
                contrib = lax.dot_general(
                    tiles_ref[i], panel_ref[fetch], (((0,), (0,)), ((), ())),
                    preferred_element_type=jnp.float32,
                )
            else:
                fetch = jnp.clip(source_ref[slot], 0, in_blocks - 1)
                target = jnp.clip(dest_ref[slot], 0, out_blocks - 1)
                contrib = jnp.dot(
                    tiles_ref[i], panel_ref[fetch], preferred_element_type=jnp.float32
                )
            out_ref[target] += contrib

        return carry

    lax.fori_loop(0, group, one_tile, 0)


def accumulate(tiles, dest_ids, source_ids, live_count, source_blocks, out_blocks, backward):
    slots, block, _ = tiles.shape
    width = source_blocks.shape[-1]
    in_blocks = source_blocks.shape[0]
    group = math.gcd(slots, GROUP)
    steps = slots // group

    def tile_map(g, dest, source, count):
        last = jnp.maximum(count[0] - 1, 0) // group
        return (jnp.minimum(g, last), 0, 0)

    flops = 2 * slots * block * block * width
    bytes_accessed = tiles.size * 2 + source_blocks.size * 2 + out_blocks * block * width * 4
    return pl.pallas_call(
        functools.partial(accumulate_kernel, backward),
        out_shape=jax.ShapeDtypeStruct((out_blocks, block, width), jnp.float32),
        grid_spec=pltpu.PrefetchScalarGridSpec(
            num_scalar_prefetch=3,
            grid=(steps,),
            in_specs=[
                pl.BlockSpec((group, block, block), tile_map),
                pl.BlockSpec((in_blocks, block, width), lambda g, d, s, c: (0, 0, 0)),
            ],
            out_specs=pl.BlockSpec((out_blocks, block, width), lambda g, d, s, c: (0, 0, 0)),
        ),
        compiler_params=pltpu.CompilerParams(
            dimension_semantics=("arbitrary",), vmem_limit_bytes=60 * 1024 * 1024
        ),
        cost_estimate=pl.CostEstimate(
            flops=flops, transcendentals=0, bytes_accessed=bytes_accessed
        ),
    )(dest_ids, source_ids, live_count.reshape(1), tiles, source_blocks)


def per_device(features, weight, bias, cotangent, tiles, tile_rows, tile_cols, tile_counts):
    tile_set = tiles[0, 0]
    dest_ids = tile_rows[0, 0]
    source_ids = tile_cols[0, 0]
    live_count = tile_counts[0, 0]
    block = tile_set.shape[-1]
    own_nodes = features.shape[0]
    width = features.shape[1]
    row_count = lax.axis_size("row")
    col_count = lax.axis_size("col")
    blocks_down = own_nodes * col_count // block
    blocks_across = own_nodes * row_count // block
    factor = 1.0 / math.sqrt(own_nodes * row_count * col_count)
    panel = lax.all_gather(features, "row", axis=0, tiled=True)
    panel_blocks = panel.reshape(blocks_across, block, width)
    partial_value = accumulate(
        tile_set, dest_ids, source_ids, live_count, panel_blocks, blocks_down, False
    )
    term = partial_value.reshape(blocks_down * block, width)
    summed = lax.psum_scatter(term, "col", scatter_dimension=0, tiled=True)
    aggregated = summed.astype(jnp.bfloat16)
    preact = jnp.dot(aggregated, weight, preferred_element_type=jnp.float32) + bias
    hidden = jax.nn.silu(preact).astype(jnp.bfloat16)
    sigma = jax.nn.sigmoid(preact)
    slope = sigma * (1.0 + preact * (1.0 - sigma))
    grad_pre = (cotangent.astype(jnp.float32) * slope).astype(jnp.bfloat16)
    local_weight = jnp.einsum("nf,ng->fg", aggregated, grad_pre, preferred_element_type=jnp.float32)
    local_bias = jnp.sum(grad_pre.astype(jnp.float32), axis=0)
    grad_agg = jnp.dot(grad_pre, weight.T, preferred_element_type=jnp.float32).astype(jnp.bfloat16)
    grad_panel = lax.all_gather(grad_agg, "col", axis=0, tiled=True)
    grad_blocks = grad_panel.reshape(blocks_down, block, width)
    partial_back = accumulate(
        tile_set, dest_ids, source_ids, live_count, grad_blocks, blocks_across, True
    )
    term_back = partial_back.reshape(blocks_across * block, width)
    grad_features = lax.psum_scatter(
        term_back.astype(jnp.bfloat16), "row", scatter_dimension=0, tiled=True
    )
    grad_weight, grad_bias = lax.psum((local_weight, local_bias), ("row", "col"))
    grad_weight = grad_weight * factor
    grad_bias = grad_bias * factor
    return (hidden, grad_weight, grad_bias, grad_features)


def solution(mesh):
    in_specs = (
        P(("col", "row"), None),
        P(),
        P(),
        P(("row", "col"), None),
        P("row", "col", None, None, None),
        P("row", "col", None),
        P("row", "col", None),
        P("row", "col"),
    )
    out_specs = (P(("row", "col"), None), P(), P(), P(("col", "row"), None))
    return jax.shard_map(
        per_device, mesh=mesh, in_specs=in_specs, out_specs=out_specs, check_vma=False
    )
```

```python
import functools
import math

import jax
import jax.numpy as jnp
from jax import lax
from jax.experimental import pallas as pl
from jax.experimental.pallas import tpu as pltpu
from jax.sharding import PartitionSpec as P

GROUP = 32


def accumulate_kernel(backward, dest_ref, source_ref, count_ref, tiles_ref, panel_ref, out_ref):
    step = pl.program_id(0)
    group = tiles_ref.shape[0]
    out_blocks = out_ref.shape[0]
    in_blocks = panel_ref.shape[0]

    @pl.when(step == 0)
    def _():
        out_ref[...] = jnp.zeros_like(out_ref)

    base = step * group
    live_count = count_ref[0]

    def one_tile(i, carry):
        slot = base + i

        @pl.when(slot < live_count)
        def _():
            if backward:
                fetch = jnp.clip(dest_ref[slot], 0, in_blocks - 1)
                target = jnp.clip(source_ref[slot], 0, out_blocks - 1)
                contrib = lax.dot_general(
                    tiles_ref[i], panel_ref[fetch], (((0,), (0,)), ((), ())),
                    preferred_element_type=jnp.float32,
                )
            else:
                fetch = jnp.clip(source_ref[slot], 0, in_blocks - 1)
                target = jnp.clip(dest_ref[slot], 0, out_blocks - 1)
                contrib = jnp.dot(
                    tiles_ref[i], panel_ref[fetch], preferred_element_type=jnp.float32
                )
            out_ref[target] += contrib

        return carry

    lax.fori_loop(0, group, one_tile, 0)


def accumulate(tiles, dest_ids, source_ids, live_count, source_blocks, out_blocks, backward):
    slots, block, _ = tiles.shape
    width = source_blocks.shape[-1]
    in_blocks = source_blocks.shape[0]
    group = math.gcd(slots, GROUP)
    steps = slots // group

    def tile_map(g, dest, source, count):
        last = jnp.maximum(count[0] - 1, 0) // group
        return (jnp.minimum(g, last), 0, 0)

    flops = 2 * slots * block * block * width
    bytes_accessed = tiles.size * 2 + source_blocks.size * 2 + out_blocks * block * width * 4
    return pl.pallas_call(
        functools.partial(accumulate_kernel, backward),
        out_shape=jax.ShapeDtypeStruct((out_blocks, block, width), jnp.float32),
        grid_spec=pltpu.PrefetchScalarGridSpec(
            num_scalar_prefetch=3,
            grid=(steps,),
            in_specs=[
                pl.BlockSpec((group, block, block), tile_map),
                pl.BlockSpec((in_blocks, block, width), lambda g, d, s, c: (0, 0, 0)),
            ],
            out_specs=pl.BlockSpec((out_blocks, block, width), lambda g, d, s, c: (0, 0, 0)),
        ),
        compiler_params=pltpu.CompilerParams(
            dimension_semantics=("arbitrary",), vmem_limit_bytes=60 * 1024 * 1024
        ),
        cost_estimate=pl.CostEstimate(
            flops=flops, transcendentals=0, bytes_accessed=bytes_accessed
        ),
    )(dest_ids, source_ids, live_count.reshape(1), tiles, source_blocks)


def butterfly_sum(value, axis):
    size = lax.axis_size(axis)
    distance = 1
    while distance < size:
        pairs = [(i, i ^ distance) for i in range(size)]
        value = value + lax.ppermute(value, axis, pairs)
        distance *= 2
    return value


def per_device(features, weight, bias, cotangent, tiles, tile_rows, tile_cols, tile_counts):
    tile_set = tiles[0, 0]
    dest_ids = tile_rows[0, 0]
    source_ids = tile_cols[0, 0]
    live_count = tile_counts[0, 0]
    block = tile_set.shape[-1]
    own_nodes = features.shape[0]
    width = features.shape[1]
    row_count = lax.axis_size("row")
    col_count = lax.axis_size("col")
    blocks_down = own_nodes * col_count // block
    blocks_across = own_nodes * row_count // block
    factor = 1.0 / math.sqrt(own_nodes * row_count * col_count)
    panel = lax.all_gather(features, "row", axis=0, tiled=True)
    panel_blocks = panel.reshape(blocks_across, block, width)
    partial_value = accumulate(
        tile_set, dest_ids, source_ids, live_count, panel_blocks, blocks_down, False
    )
    term = partial_value.reshape(blocks_down * block, width)
    summed = lax.psum_scatter(term.astype(jnp.bfloat16), "col", scatter_dimension=0, tiled=True)
    aggregated = summed.astype(jnp.bfloat16)
    preact = jnp.dot(aggregated, weight, preferred_element_type=jnp.float32) + bias
    hidden = jax.nn.silu(preact).astype(jnp.bfloat16)
    sigma = jax.nn.sigmoid(preact)
    slope = sigma * (1.0 + preact * (1.0 - sigma))
    grad_pre = (cotangent.astype(jnp.float32) * slope).astype(jnp.bfloat16)
    local_weight = jnp.einsum("nf,ng->fg", aggregated, grad_pre, preferred_element_type=jnp.float32)
    local_bias = jnp.sum(grad_pre.astype(jnp.float32), axis=0)
    grad_agg = jnp.dot(grad_pre, weight.T, preferred_element_type=jnp.float32).astype(jnp.bfloat16)
    grad_panel = lax.all_gather(grad_agg, "col", axis=0, tiled=True)
    grad_blocks = grad_panel.reshape(blocks_down, block, width)
    partial_back = accumulate(
        tile_set, dest_ids, source_ids, live_count, grad_blocks, blocks_across, True
    )
    term_back = partial_back.reshape(blocks_across * block, width)
    grad_features = lax.psum_scatter(
        term_back.astype(jnp.bfloat16), "row", scatter_dimension=0, tiled=True
    )
    packed = jnp.concatenate([local_weight, local_bias[None, :]], axis=0)
    packed = butterfly_sum(butterfly_sum(packed, "col"), "row")
    grad_weight = packed[:width] * factor
    grad_bias = packed[width] * factor
    return (hidden, grad_weight, grad_bias, grad_features)


def solution(mesh):
    in_specs = (
        P(("col", "row"), None),
        P(),
        P(),
        P(("row", "col"), None),
        P("row", "col", None, None, None),
        P("row", "col", None),
        P("row", "col", None),
        P("row", "col"),
    )
    out_specs = (P(("row", "col"), None), P(), P(), P(("col", "row"), None))
    return jax.shard_map(
        per_device, mesh=mesh, in_specs=in_specs, out_specs=out_specs, check_vma=False
    )
```

```python
import functools
import math

import jax
import jax.numpy as jnp
from jax import lax
from jax.experimental import pallas as pl
from jax.experimental.pallas import tpu as pltpu
from jax.sharding import PartitionSpec as P

GROUP = 32


def accumulate_kernel(backward, dest_ref, source_ref, count_ref, tiles_ref, panel_ref, out_ref):
    step = pl.program_id(0)
    group = tiles_ref.shape[0]
    out_blocks = out_ref.shape[0]
    in_blocks = panel_ref.shape[0]

    @pl.when(step == 0)
    def _():
        out_ref[...] = jnp.zeros_like(out_ref)

    base = step * group
    live_count = count_ref[0]

    def one_tile(i, carry):
        slot = base + i

        @pl.when(slot < live_count)
        def _():
            if backward:
                fetch = jnp.clip(dest_ref[slot], 0, in_blocks - 1)
                target = jnp.clip(source_ref[slot], 0, out_blocks - 1)
                contrib = lax.dot_general(
                    tiles_ref[i], panel_ref[fetch], (((0,), (0,)), ((), ())),
                    preferred_element_type=jnp.float32,
                )
            else:
                fetch = jnp.clip(source_ref[slot], 0, in_blocks - 1)
                target = jnp.clip(dest_ref[slot], 0, out_blocks - 1)
                contrib = jnp.dot(
                    tiles_ref[i], panel_ref[fetch], preferred_element_type=jnp.float32
                )
            out_ref[target] += contrib

        return carry

    lax.fori_loop(0, group, one_tile, 0)


def accumulate(tiles, dest_ids, source_ids, live_count, source_blocks, out_blocks, backward):
    slots, block, _ = tiles.shape
    width = source_blocks.shape[-1]
    in_blocks = source_blocks.shape[0]
    group = math.gcd(slots, GROUP)
    steps = slots // group

    def tile_map(g, dest, source, count):
        last = jnp.maximum(count[0] - 1, 0) // group
        return (jnp.minimum(g, last), 0, 0)

    flops = 2 * slots * block * block * width
    bytes_accessed = tiles.size * 2 + source_blocks.size * 2 + out_blocks * block * width * 4
    return pl.pallas_call(
        functools.partial(accumulate_kernel, backward),
        out_shape=jax.ShapeDtypeStruct((out_blocks, block, width), jnp.float32),
        grid_spec=pltpu.PrefetchScalarGridSpec(
            num_scalar_prefetch=3,
            grid=(steps,),
            in_specs=[
                pl.BlockSpec((group, block, block), tile_map),
                pl.BlockSpec((in_blocks, block, width), lambda g, d, s, c: (0, 0, 0)),
            ],
            out_specs=pl.BlockSpec((out_blocks, block, width), lambda g, d, s, c: (0, 0, 0)),
        ),
        compiler_params=pltpu.CompilerParams(
            dimension_semantics=("arbitrary",), vmem_limit_bytes=60 * 1024 * 1024
        ),
        cost_estimate=pl.CostEstimate(
            flops=flops, transcendentals=0, bytes_accessed=bytes_accessed
        ),
    )(dest_ids, source_ids, live_count.reshape(1), tiles, source_blocks)


def butterfly_sum(value, axis):
    size = lax.axis_size(axis)
    distance = 1
    while distance < size:
        pairs = [(i, i ^ distance) for i in range(size)]
        value = value + lax.ppermute(value, axis, pairs)
        distance *= 2
    return value


def gather_all(value, axis, size):
    spread = jnp.broadcast_to(value[None], (size,) + value.shape)
    got = lax.all_to_all(spread, axis, 0, 0, tiled=False)
    return got.reshape((size * value.shape[0],) + value.shape[1:])


def scatter_sum(value, axis, size):
    parts = value.reshape((size, value.shape[0] // size) + value.shape[1:])
    got = lax.all_to_all(parts, axis, 0, 0, tiled=False)
    return jnp.sum(got.astype(jnp.float32), axis=0)


def per_device(features, weight, bias, cotangent, tiles, tile_rows, tile_cols, tile_counts):
    tile_set = tiles[0, 0]
    dest_ids = tile_rows[0, 0]
    source_ids = tile_cols[0, 0]
    live_count = tile_counts[0, 0]
    block = tile_set.shape[-1]
    own_nodes = features.shape[0]
    width = features.shape[1]
    row_count = lax.axis_size("row")
    col_count = lax.axis_size("col")
    blocks_down = own_nodes * col_count // block
    blocks_across = own_nodes * row_count // block
    factor = 1.0 / math.sqrt(own_nodes * row_count * col_count)
    panel = gather_all(features, "row", row_count)
    panel_blocks = panel.reshape(blocks_across, block, width)
    partial_value = accumulate(
        tile_set, dest_ids, source_ids, live_count, panel_blocks, blocks_down, False
    )
    term = partial_value.reshape(blocks_down * block, width)
    summed = scatter_sum(term, "col", col_count)
    aggregated = summed.astype(jnp.bfloat16)
    preact = jnp.dot(aggregated, weight, preferred_element_type=jnp.float32) + bias
    hidden = jax.nn.silu(preact).astype(jnp.bfloat16)
    sigma = jax.nn.sigmoid(preact)
    slope = sigma * (1.0 + preact * (1.0 - sigma))
    grad_pre = (cotangent.astype(jnp.float32) * slope).astype(jnp.bfloat16)
    local_weight = jnp.einsum("nf,ng->fg", aggregated, grad_pre, preferred_element_type=jnp.float32)
    local_bias = jnp.sum(grad_pre.astype(jnp.float32), axis=0)
    grad_agg = jnp.dot(grad_pre, weight.T, preferred_element_type=jnp.float32).astype(jnp.bfloat16)
    grad_panel = gather_all(grad_agg, "col", col_count)
    grad_blocks = grad_panel.reshape(blocks_down, block, width)
    partial_back = accumulate(
        tile_set, dest_ids, source_ids, live_count, grad_blocks, blocks_across, True
    )
    term_back = partial_back.reshape(blocks_across * block, width)
    grad_features = scatter_sum(term_back.astype(jnp.bfloat16), "row", row_count).astype(
        jnp.bfloat16
    )
    packed = jnp.concatenate([local_weight, local_bias[None, :]], axis=0)
    packed = butterfly_sum(butterfly_sum(packed, "col"), "row")
    grad_weight = packed[:width] * factor
    grad_bias = packed[width] * factor
    return (hidden, grad_weight, grad_bias, grad_features)


def solution(mesh):
    in_specs = (
        P(("col", "row"), None),
        P(),
        P(),
        P(("row", "col"), None),
        P("row", "col", None, None, None),
        P("row", "col", None),
        P("row", "col", None),
        P("row", "col"),
    )
    out_specs = (P(("row", "col"), None), P(), P(), P(("col", "row"), None))
    return jax.shard_map(
        per_device, mesh=mesh, in_specs=in_specs, out_specs=out_specs, check_vma=False
    )
```

```python
import functools
import math

import jax
import jax.numpy as jnp
from jax import lax
from jax.experimental import pallas as pl
from jax.experimental.pallas import tpu as pltpu
from jax.sharding import PartitionSpec as P

GROUP = 32


def accumulate_kernel(backward, dest_ref, source_ref, count_ref, tiles_ref, panel_ref, out_ref):
    step = pl.program_id(0)
    group = tiles_ref.shape[0]
    out_blocks = out_ref.shape[0]
    in_blocks = panel_ref.shape[0]

    @pl.when(step == 0)
    def _():
        out_ref[...] = jnp.zeros_like(out_ref)

    base = step * group
    live_count = count_ref[0]

    def one_tile(i, carry):
        slot = base + i

        @pl.when(slot < live_count)
        def _():
            if backward:
                fetch = jnp.clip(dest_ref[slot], 0, in_blocks - 1)
                target = jnp.clip(source_ref[slot], 0, out_blocks - 1)
                contrib = lax.dot_general(
                    tiles_ref[i], panel_ref[fetch], (((0,), (0,)), ((), ())),
                    preferred_element_type=jnp.float32,
                )
            else:
                fetch = jnp.clip(source_ref[slot], 0, in_blocks - 1)
                target = jnp.clip(dest_ref[slot], 0, out_blocks - 1)
                contrib = jnp.dot(
                    tiles_ref[i], panel_ref[fetch], preferred_element_type=jnp.float32
                )
            out_ref[target] += contrib

        return carry

    lax.fori_loop(0, group, one_tile, 0)


def accumulate(tiles, dest_ids, source_ids, live_count, source_blocks, out_blocks, backward):
    slots, block, _ = tiles.shape
    width = source_blocks.shape[-1]
    in_blocks = source_blocks.shape[0]
    group = math.gcd(slots, GROUP)
    steps = slots // group

    def tile_map(g, dest, source, count):
        last = jnp.maximum(count[0] - 1, 0) // group
        return (jnp.minimum(g, last), 0, 0)

    flops = 2 * slots * block * block * width
    bytes_accessed = tiles.size * 2 + source_blocks.size * 2 + out_blocks * block * width * 4
    return pl.pallas_call(
        functools.partial(accumulate_kernel, backward),
        out_shape=jax.ShapeDtypeStruct((out_blocks, block, width), jnp.float32),
        grid_spec=pltpu.PrefetchScalarGridSpec(
            num_scalar_prefetch=3,
            grid=(steps,),
            in_specs=[
                pl.BlockSpec((group, block, block), tile_map),
                pl.BlockSpec((in_blocks, block, width), lambda g, d, s, c: (0, 0, 0)),
            ],
            out_specs=pl.BlockSpec((out_blocks, block, width), lambda g, d, s, c: (0, 0, 0)),
        ),
        compiler_params=pltpu.CompilerParams(
            dimension_semantics=("arbitrary",), vmem_limit_bytes=60 * 1024 * 1024
        ),
        cost_estimate=pl.CostEstimate(
            flops=flops, transcendentals=0, bytes_accessed=bytes_accessed
        ),
    )(dest_ids, source_ids, live_count.reshape(1), tiles, source_blocks)


def butterfly_sum(value, axis):
    size = lax.axis_size(axis)
    distance = 1
    while distance < size:
        pairs = [(i, i ^ distance) for i in range(size)]
        value = value + lax.ppermute(value, axis, pairs)
        distance *= 2
    return value


def gather_all(value, axis, size):
    spread = jnp.broadcast_to(value[None], (size,) + value.shape)
    got = lax.all_to_all(spread, axis, 0, 0, tiled=False)
    return got.reshape((size * value.shape[0],) + value.shape[1:])


def scatter_sum(value, axis, size):
    parts = value.reshape((size, value.shape[0] // size) + value.shape[1:])
    got = lax.all_to_all(parts, axis, 0, 0, tiled=False)
    return jnp.sum(got.astype(jnp.float32), axis=0)


def per_device(features, weight, bias, cotangent, tiles, tile_rows, tile_cols, tile_counts):
    tile_set = tiles[0, 0]
    dest_ids = tile_rows[0, 0]
    source_ids = tile_cols[0, 0]
    live_count = tile_counts[0, 0]
    block = tile_set.shape[-1]
    own_nodes = features.shape[0]
    width = features.shape[1]
    row_count = lax.axis_size("row")
    col_count = lax.axis_size("col")
    blocks_down = own_nodes * col_count // block
    blocks_across = own_nodes * row_count // block
    factor = 1.0 / math.sqrt(own_nodes * row_count * col_count)
    panel = gather_all(features, "row", row_count)
    panel_blocks = panel.reshape(blocks_across, block, width)
    partial_value = accumulate(
        tile_set, dest_ids, source_ids, live_count, panel_blocks, blocks_down, False
    )
    term = partial_value.reshape(blocks_down * block, width)
    summed = scatter_sum(term.astype(jnp.bfloat16), "col", col_count)
    aggregated = summed.astype(jnp.bfloat16)
    preact = jnp.dot(aggregated, weight, preferred_element_type=jnp.float32) + bias
    hidden = jax.nn.silu(preact).astype(jnp.bfloat16)
    sigma = jax.nn.sigmoid(preact)
    slope = sigma * (1.0 + preact * (1.0 - sigma))
    grad_pre = (cotangent.astype(jnp.float32) * slope).astype(jnp.bfloat16)
    local_weight = jnp.einsum("nf,ng->fg", aggregated, grad_pre, preferred_element_type=jnp.float32)
    local_bias = jnp.sum(grad_pre.astype(jnp.float32), axis=0)
    grad_agg = jnp.dot(grad_pre, weight.T, preferred_element_type=jnp.float32).astype(jnp.bfloat16)
    packed = jnp.concatenate([local_weight, local_bias[None, :]], axis=0)
    grad_panel = lax.all_gather(grad_agg, "col", axis=0, tiled=True)
    packed = butterfly_sum(butterfly_sum(packed, "col"), "row")
    grad_panel, packed = lax.optimization_barrier((grad_panel, packed))
    grad_blocks = grad_panel.reshape(blocks_down, block, width)
    partial_back = accumulate(
        tile_set, dest_ids, source_ids, live_count, grad_blocks, blocks_across, True
    )
    term_back = partial_back.reshape(blocks_across * block, width)
    grad_features = scatter_sum(term_back.astype(jnp.bfloat16), "row", row_count).astype(
        jnp.bfloat16
    )
    grad_weight = packed[:width] * factor
    grad_bias = packed[width] * factor
    return (hidden, grad_weight, grad_bias, grad_features)


def solution(mesh):
    in_specs = (
        P(("col", "row"), None),
        P(),
        P(),
        P(("row", "col"), None),
        P("row", "col", None, None, None),
        P("row", "col", None),
        P("row", "col", None),
        P("row", "col"),
    )
    out_specs = (P(("row", "col"), None), P(), P(), P(("col", "row"), None))
    return jax.shard_map(
        per_device, mesh=mesh, in_specs=in_specs, out_specs=out_specs, check_vma=False
    )
```

```python
import functools
import math

import jax
import jax.numpy as jnp
from jax import lax
from jax.experimental import pallas as pl
from jax.experimental.pallas import tpu as pltpu
from jax.sharding import PartitionSpec as P

GROUP = 32
UNROLL = 32


def accumulate_kernel(backward, dest_ref, source_ref, count_ref, tiles_ref, panel_ref, out_ref):
    step = pl.program_id(0)
    group = tiles_ref.shape[0]
    out_blocks = out_ref.shape[0]
    in_blocks = panel_ref.shape[0]

    @pl.when(step == 0)
    def _():
        out_ref[...] = jnp.zeros_like(out_ref)

    base = step * group
    live_count = count_ref[0]

    def one_tile(i, checked):
        slot = base + i
        if backward:
            fetch = jnp.clip(dest_ref[slot], 0, in_blocks - 1)
            target = jnp.clip(source_ref[slot], 0, out_blocks - 1)
            contrib = lax.dot_general(
                tiles_ref[i], panel_ref[fetch], (((0,), (0,)), ((), ())),
                preferred_element_type=jnp.float32,
            )
        else:
            fetch = jnp.clip(source_ref[slot], 0, in_blocks - 1)
            target = jnp.clip(dest_ref[slot], 0, out_blocks - 1)
            contrib = jnp.dot(
                tiles_ref[i], panel_ref[fetch], preferred_element_type=jnp.float32
            )
        if checked:
            contrib = jnp.where(slot < live_count, contrib, 0.0)
        out_ref[target] += contrib

    @pl.when(base + group <= live_count)
    def _():
        @pl.loop(0, group, unroll=UNROLL)
        def _(i):
            one_tile(i, False)

    @pl.when((base < live_count) & (base + group > live_count))
    def _():
        @pl.loop(0, group)
        def _(i):
            one_tile(i, True)


def accumulate(tiles, dest_ids, source_ids, live_count, source_blocks, out_blocks, backward):
    slots, block, _ = tiles.shape
    width = source_blocks.shape[-1]
    in_blocks = source_blocks.shape[0]
    group = math.gcd(slots, GROUP)
    steps = slots // group

    def tile_map(g, dest, source, count):
        last = jnp.maximum(count[0] - 1, 0) // group
        return (jnp.minimum(g, last), 0, 0)

    flops = 2 * slots * block * block * width
    bytes_accessed = tiles.size * 2 + source_blocks.size * 2 + out_blocks * block * width * 4
    return pl.pallas_call(
        functools.partial(accumulate_kernel, backward),
        out_shape=jax.ShapeDtypeStruct((out_blocks, block, width), jnp.float32),
        grid_spec=pltpu.PrefetchScalarGridSpec(
            num_scalar_prefetch=3,
            grid=(steps,),
            in_specs=[
                pl.BlockSpec((group, block, block), tile_map),
                pl.BlockSpec((in_blocks, block, width), lambda g, d, s, c: (0, 0, 0)),
            ],
            out_specs=pl.BlockSpec((out_blocks, block, width), lambda g, d, s, c: (0, 0, 0)),
        ),
        compiler_params=pltpu.CompilerParams(
            dimension_semantics=("arbitrary",), vmem_limit_bytes=60 * 1024 * 1024
        ),
        cost_estimate=pl.CostEstimate(
            flops=flops, transcendentals=0, bytes_accessed=bytes_accessed
        ),
    )(dest_ids, source_ids, live_count.reshape(1), tiles, source_blocks)


def butterfly_sum(value, axis):
    size = lax.axis_size(axis)
    distance = 1
    while distance < size:
        pairs = [(i, i ^ distance) for i in range(size)]
        value = value + lax.ppermute(value, axis, pairs)
        distance *= 2
    return value


def gather_all(value, axis, size):
    spread = jnp.broadcast_to(value[None], (size,) + value.shape)
    got = lax.all_to_all(spread, axis, 0, 0, tiled=False)
    return got.reshape((size * value.shape[0],) + value.shape[1:])


def scatter_sum(value, axis, size):
    parts = value.reshape((size, value.shape[0] // size) + value.shape[1:])
    got = lax.all_to_all(parts, axis, 0, 0, tiled=False)
    return jnp.sum(got.astype(jnp.float32), axis=0)


def per_device(features, weight, bias, cotangent, tiles, tile_rows, tile_cols, tile_counts):
    tile_set = tiles[0, 0]
    dest_ids = tile_rows[0, 0]
    source_ids = tile_cols[0, 0]
    live_count = tile_counts[0, 0]
    block = tile_set.shape[-1]
    own_nodes = features.shape[0]
    width = features.shape[1]
    row_count = lax.axis_size("row")
    col_count = lax.axis_size("col")
    blocks_down = own_nodes * col_count // block
    blocks_across = own_nodes * row_count // block
    factor = 1.0 / math.sqrt(own_nodes * row_count * col_count)
    panel = gather_all(features, "row", row_count)
    panel_blocks = panel.reshape(blocks_across, block, width)
    partial_value = accumulate(
        tile_set, dest_ids, source_ids, live_count, panel_blocks, blocks_down, False
    )
    term = partial_value.reshape(blocks_down * block, width)
    summed = scatter_sum(term.astype(jnp.bfloat16), "col", col_count)
    aggregated = summed.astype(jnp.bfloat16)
    preact = jnp.dot(aggregated, weight, preferred_element_type=jnp.float32) + bias
    hidden = jax.nn.silu(preact).astype(jnp.bfloat16)
    sigma = jax.nn.sigmoid(preact)
    slope = sigma * (1.0 + preact * (1.0 - sigma))
    grad_pre = (cotangent.astype(jnp.float32) * slope).astype(jnp.bfloat16)
    local_weight = jnp.einsum("nf,ng->fg", aggregated, grad_pre, preferred_element_type=jnp.float32)
    local_bias = jnp.sum(grad_pre.astype(jnp.float32), axis=0)
    grad_agg = jnp.dot(grad_pre, weight.T, preferred_element_type=jnp.float32).astype(jnp.bfloat16)
    packed = jnp.concatenate([local_weight, local_bias[None, :]], axis=0)
    grad_panel = lax.all_gather(grad_agg, "col", axis=0, tiled=True)
    packed = butterfly_sum(butterfly_sum(packed, "col"), "row")
    grad_panel, packed = lax.optimization_barrier((grad_panel, packed))
    grad_blocks = grad_panel.reshape(blocks_down, block, width)
    partial_back = accumulate(
        tile_set, dest_ids, source_ids, live_count, grad_blocks, blocks_across, True
    )
    term_back = partial_back.reshape(blocks_across * block, width)
    grad_features = scatter_sum(term_back.astype(jnp.bfloat16), "row", row_count).astype(
        jnp.bfloat16
    )
    grad_weight = packed[:width] * factor
    grad_bias = packed[width] * factor
    return (hidden, grad_weight, grad_bias, grad_features)


def solution(mesh):
    in_specs = (
        P(("col", "row"), None),
        P(),
        P(),
        P(("row", "col"), None),
        P("row", "col", None, None, None),
        P("row", "col", None),
        P("row", "col", None),
        P("row", "col"),
    )
    out_specs = (P(("row", "col"), None), P(), P(), P(("col", "row"), None))
    return jax.shard_map(
        per_device, mesh=mesh, in_specs=in_specs, out_specs=out_specs, check_vma=False
    )
```

```python
import functools
import math

import jax
import jax.numpy as jnp
from jax import lax
from jax.experimental import pallas as pl
from jax.experimental.pallas import tpu as pltpu
from jax.sharding import PartitionSpec as P

GROUP = 32
UNROLL = 32


def accumulate_kernel(backward, dest_ref, source_ref, count_ref, tiles_ref, panel_ref, out_ref):
    step = pl.program_id(0)
    group = tiles_ref.shape[0]
    out_blocks = out_ref.shape[0]
    in_blocks = panel_ref.shape[0]

    @pl.when(step == 0)
    def _():
        out_ref[...] = jnp.zeros_like(out_ref)

    base = step * group
    live_count = count_ref[0]

    def one_tile(i, checked):
        slot = base + i
        if backward:
            fetch = jnp.clip(dest_ref[slot], 0, in_blocks - 1)
            target = jnp.clip(source_ref[slot], 0, out_blocks - 1)
            contrib = lax.dot_general(
                tiles_ref[i], panel_ref[fetch], (((0,), (0,)), ((), ())),
                preferred_element_type=jnp.float32,
            )
        else:
            fetch = jnp.clip(source_ref[slot], 0, in_blocks - 1)
            target = jnp.clip(dest_ref[slot], 0, out_blocks - 1)
            contrib = jnp.dot(
                tiles_ref[i], panel_ref[fetch], preferred_element_type=jnp.float32
            )
        if checked:
            contrib = jnp.where(slot < live_count, contrib, 0.0)
        out_ref[target] += contrib

    @pl.when(base + group <= live_count)
    def _():
        @pl.loop(0, group, unroll=UNROLL)
        def _(i):
            one_tile(i, False)

    @pl.when((base < live_count) & (base + group > live_count))
    def _():
        @pl.loop(0, group)
        def _(i):
            one_tile(i, True)


def accumulate(tiles, dest_ids, source_ids, live_count, source_blocks, out_blocks, backward):
    slots, block, _ = tiles.shape
    width = source_blocks.shape[-1]
    in_blocks = source_blocks.shape[0]
    group = math.gcd(slots, GROUP)
    steps = slots // group

    def tile_map(g, dest, source, count):
        last = jnp.maximum(count[0] - 1, 0) // group
        return (jnp.minimum(g, last), 0, 0)

    flops = 2 * slots * block * block * width
    bytes_accessed = tiles.size * 2 + source_blocks.size * 2 + out_blocks * block * width * 4
    return pl.pallas_call(
        functools.partial(accumulate_kernel, backward),
        out_shape=jax.ShapeDtypeStruct((out_blocks, block, width), jnp.float32),
        grid_spec=pltpu.PrefetchScalarGridSpec(
            num_scalar_prefetch=3,
            grid=(steps,),
            in_specs=[
                pl.BlockSpec((group, block, block), tile_map),
                pl.BlockSpec((in_blocks, block, width), lambda g, d, s, c: (0, 0, 0)),
            ],
            out_specs=pl.BlockSpec((out_blocks, block, width), lambda g, d, s, c: (0, 0, 0)),
        ),
        compiler_params=pltpu.CompilerParams(
            dimension_semantics=("arbitrary",), vmem_limit_bytes=60 * 1024 * 1024
        ),
        cost_estimate=pl.CostEstimate(
            flops=flops, transcendentals=0, bytes_accessed=bytes_accessed
        ),
    )(dest_ids, source_ids, live_count.reshape(1), tiles, source_blocks)


def butterfly_sum(value, axis):
    size = lax.axis_size(axis)
    distance = 1
    while distance < size:
        pairs = [(i, i ^ distance) for i in range(size)]
        value = value + lax.ppermute(value, axis, pairs)
        distance *= 2
    return value


def exchange_kernel(axis, size, spread, parts_ref, out_ref, local_sem, send_sems, recv_sems):
    me = lax.axis_index(axis)
    barrier = pltpu.get_barrier_semaphore()
    for shift in range(1, size):
        pl.semaphore_signal(
            barrier, 1, device_id={axis: lax.rem(me + shift, size)},
            device_id_type=pl.DeviceIdType.MESH,
        )
    pl.semaphore_wait(barrier, size - 1)
    copies = []
    for shift in range(1, size):
        peer = lax.rem(me + shift, size)
        copy = pltpu.make_async_remote_copy(
            src_ref=parts_ref if spread else parts_ref.at[peer],
            dst_ref=out_ref.at[me],
            send_sem=send_sems.at[shift],
            recv_sem=recv_sems.at[shift],
            device_id={axis: peer},
            device_id_type=pl.DeviceIdType.MESH,
        )
        copy.start()
        copies.append(copy)
    local = pltpu.make_async_copy(
        parts_ref if spread else parts_ref.at[me], out_ref.at[me], local_sem
    )
    local.start()
    local.wait()
    for copy in copies:
        copy.wait_send()
        copy.wait_recv()


def exchange(parts, axis, size, spread, tag):
    shape = (size,) + parts.shape[1 - spread:]
    nbytes = math.prod(shape) * parts.dtype.itemsize
    return pl.pallas_call(
        functools.partial(exchange_kernel, axis, size, spread),
        out_shape=jax.ShapeDtypeStruct(shape, parts.dtype),
        in_specs=[pl.BlockSpec(memory_space=pl.ANY)],
        out_specs=pl.BlockSpec(memory_space=pl.ANY),
        scratch_shapes=[
            pltpu.SemaphoreType.DMA,
            pltpu.SemaphoreType.DMA((size,)),
            pltpu.SemaphoreType.DMA((size,)),
        ],
        compiler_params=pltpu.CompilerParams(collective_id=tag, has_side_effects=True),
        cost_estimate=pl.CostEstimate(flops=0, transcendentals=0, bytes_accessed=2 * nbytes),
    )(parts)


def gather_all(value, axis, size, tag):
    got = exchange(value, axis, size, True, tag)
    return got.reshape((size * value.shape[0],) + value.shape[1:])


def scatter_sum(value, axis, size, tag):
    parts = value.reshape((size, value.shape[0] // size) + value.shape[1:])
    got = exchange(parts, axis, size, False, tag)
    return jnp.sum(got.astype(jnp.float32), axis=0)


def per_device(features, weight, bias, cotangent, tiles, tile_rows, tile_cols, tile_counts):
    tile_set = tiles[0, 0]
    dest_ids = tile_rows[0, 0]
    source_ids = tile_cols[0, 0]
    live_count = tile_counts[0, 0]
    block = tile_set.shape[-1]
    own_nodes = features.shape[0]
    width = features.shape[1]
    row_count = lax.axis_size("row")
    col_count = lax.axis_size("col")
    blocks_down = own_nodes * col_count // block
    blocks_across = own_nodes * row_count // block
    factor = 1.0 / math.sqrt(own_nodes * row_count * col_count)
    panel = gather_all(features, "row", row_count, 0)
    panel_blocks = panel.reshape(blocks_across, block, width)
    partial_value = accumulate(
        tile_set, dest_ids, source_ids, live_count, panel_blocks, blocks_down, False
    )
    term = partial_value.reshape(blocks_down * block, width)
    summed = scatter_sum(term.astype(jnp.bfloat16), "col", col_count, 1)
    aggregated = summed.astype(jnp.bfloat16)
    preact = jnp.dot(aggregated, weight, preferred_element_type=jnp.float32) + bias
    hidden = jax.nn.silu(preact).astype(jnp.bfloat16)
    sigma = jax.nn.sigmoid(preact)
    slope = sigma * (1.0 + preact * (1.0 - sigma))
    grad_pre = (cotangent.astype(jnp.float32) * slope).astype(jnp.bfloat16)
    local_weight = jnp.einsum("nf,ng->fg", aggregated, grad_pre, preferred_element_type=jnp.float32)
    local_bias = jnp.sum(grad_pre.astype(jnp.float32), axis=0)
    grad_agg = jnp.dot(grad_pre, weight.T, preferred_element_type=jnp.float32).astype(jnp.bfloat16)
    packed = jnp.concatenate([local_weight, local_bias[None, :]], axis=0)
    grad_panel = lax.all_gather(grad_agg, "col", axis=0, tiled=True)
    packed = butterfly_sum(butterfly_sum(packed, "col"), "row")
    grad_panel, packed = lax.optimization_barrier((grad_panel, packed))
    grad_blocks = grad_panel.reshape(blocks_down, block, width)
    partial_back = accumulate(
        tile_set, dest_ids, source_ids, live_count, grad_blocks, blocks_across, True
    )
    term_back = partial_back.reshape(blocks_across * block, width)
    grad_features = scatter_sum(term_back.astype(jnp.bfloat16), "row", row_count, 2).astype(
        jnp.bfloat16
    )
    grad_weight = packed[:width] * factor
    grad_bias = packed[width] * factor
    return (hidden, grad_weight, grad_bias, grad_features)


def solution(mesh):
    in_specs = (
        P(("col", "row"), None),
        P(),
        P(),
        P(("row", "col"), None),
        P("row", "col", None, None, None),
        P("row", "col", None),
        P("row", "col", None),
        P("row", "col"),
    )
    out_specs = (P(("row", "col"), None), P(), P(), P(("col", "row"), None))
    return jax.shard_map(
        per_device, mesh=mesh, in_specs=in_specs, out_specs=out_specs, check_vma=False
    )
```

```python
import functools
import math

import jax
import jax.numpy as jnp
from jax import lax
from jax.experimental import pallas as pl
from jax.experimental.pallas import tpu as pltpu
from jax.sharding import PartitionSpec as P

GROUP = 32
UNROLL = 32


def accumulate_kernel(backward, dest_ref, source_ref, count_ref, tiles_ref, panel_ref, out_ref):
    step = pl.program_id(0)
    group = tiles_ref.shape[0]
    out_blocks = out_ref.shape[0]
    in_blocks = panel_ref.shape[0]

    @pl.when(step == 0)
    def _():
        out_ref[...] = jnp.zeros_like(out_ref)

    base = step * group
    live_count = count_ref[0]

    def one_tile(i, checked):
        slot = base + i
        if backward:
            fetch = jnp.clip(dest_ref[slot], 0, in_blocks - 1)
            target = jnp.clip(source_ref[slot], 0, out_blocks - 1)
            contrib = lax.dot_general(
                tiles_ref[i], panel_ref[fetch], (((0,), (0,)), ((), ())),
                preferred_element_type=jnp.float32,
            )
        else:
            fetch = jnp.clip(source_ref[slot], 0, in_blocks - 1)
            target = jnp.clip(dest_ref[slot], 0, out_blocks - 1)
            contrib = jnp.dot(
                tiles_ref[i], panel_ref[fetch], preferred_element_type=jnp.float32
            )
        if checked:
            contrib = jnp.where(slot < live_count, contrib, 0.0)
        out_ref[target] += contrib

    @pl.when(base + group <= live_count)
    def _():
        @pl.loop(0, group, unroll=UNROLL)
        def _(i):
            one_tile(i, False)

    @pl.when((base < live_count) & (base + group > live_count))
    def _():
        @pl.loop(0, group)
        def _(i):
            one_tile(i, True)


def accumulate(tiles, dest_ids, source_ids, live_count, source_blocks, out_blocks, backward):
    slots, block, _ = tiles.shape
    width = source_blocks.shape[-1]
    in_blocks = source_blocks.shape[0]
    group = math.gcd(slots, GROUP)
    steps = slots // group

    def tile_map(g, dest, source, count):
        last = jnp.maximum(count[0] - 1, 0) // group
        return (jnp.minimum(g, last), 0, 0)

    flops = 2 * slots * block * block * width
    bytes_accessed = tiles.size * 2 + source_blocks.size * 2 + out_blocks * block * width * 4
    return pl.pallas_call(
        functools.partial(accumulate_kernel, backward),
        out_shape=jax.ShapeDtypeStruct((out_blocks, block, width), jnp.float32),
        grid_spec=pltpu.PrefetchScalarGridSpec(
            num_scalar_prefetch=3,
            grid=(steps,),
            in_specs=[
                pl.BlockSpec((group, block, block), tile_map),
                pl.BlockSpec((in_blocks, block, width), lambda g, d, s, c: (0, 0, 0)),
            ],
            out_specs=pl.BlockSpec((out_blocks, block, width), lambda g, d, s, c: (0, 0, 0)),
        ),
        compiler_params=pltpu.CompilerParams(
            dimension_semantics=("arbitrary",), vmem_limit_bytes=60 * 1024 * 1024
        ),
        cost_estimate=pl.CostEstimate(
            flops=flops, transcendentals=0, bytes_accessed=bytes_accessed
        ),
    )(dest_ids, source_ids, live_count.reshape(1), tiles, source_blocks)


def butterfly_kernel(steps, value_ref, out_ref, slots, send_sems, recv_sems):
    partners = []
    for axis, distance in steps:
        me = lax.axis_index(axis)
        bit = (me // distance) % 2
        partners.append((axis, me + distance - 2 * distance * bit))
    barrier = pltpu.get_barrier_semaphore()
    for axis, partner in partners:
        pl.semaphore_signal(
            barrier, 1, device_id={axis: partner}, device_id_type=pl.DeviceIdType.MESH
        )
    pl.semaphore_wait(barrier, len(partners))
    out_ref[...] = value_ref[...]
    for index, (axis, partner) in enumerate(partners):
        copy = pltpu.make_async_remote_copy(
            src_ref=out_ref,
            dst_ref=slots.at[index],
            send_sem=send_sems.at[index],
            recv_sem=recv_sems.at[index],
            device_id={axis: partner},
            device_id_type=pl.DeviceIdType.MESH,
        )
        copy.start()
        copy.wait_send()
        copy.wait_recv()
        out_ref[...] = out_ref[...] + slots[index]


def butterfly_sum(value, axes, tag):
    steps = []
    for axis, size in axes:
        distance = 1
        while distance < size:
            steps.append((axis, distance))
            distance *= 2
    count = len(steps)
    return pl.pallas_call(
        functools.partial(butterfly_kernel, tuple(steps)),
        out_shape=jax.ShapeDtypeStruct(value.shape, value.dtype),
        in_specs=[pl.BlockSpec(memory_space=pltpu.VMEM)],
        out_specs=pl.BlockSpec(memory_space=pltpu.VMEM),
        scratch_shapes=[
            pltpu.VMEM((count,) + value.shape, value.dtype),
            pltpu.SemaphoreType.DMA((count,)),
            pltpu.SemaphoreType.DMA((count,)),
        ],
        compiler_params=pltpu.CompilerParams(collective_id=tag, has_side_effects=True),
    )(value)


def exchange_kernel(axis, size, spread, parts_ref, out_ref, local_sem, send_sems, recv_sems):
    me = lax.axis_index(axis)
    barrier = pltpu.get_barrier_semaphore()
    for shift in range(1, size):
        pl.semaphore_signal(
            barrier, 1, device_id={axis: lax.rem(me + shift, size)},
            device_id_type=pl.DeviceIdType.MESH,
        )
    pl.semaphore_wait(barrier, size - 1)
    copies = []
    for shift in range(1, size):
        peer = lax.rem(me + shift, size)
        copy = pltpu.make_async_remote_copy(
            src_ref=parts_ref if spread else parts_ref.at[peer],
            dst_ref=out_ref.at[me],
            send_sem=send_sems.at[shift],
            recv_sem=recv_sems.at[shift],
            device_id={axis: peer},
            device_id_type=pl.DeviceIdType.MESH,
        )
        copy.start()
        copies.append(copy)
    local = pltpu.make_async_copy(
        parts_ref if spread else parts_ref.at[me], out_ref.at[me], local_sem
    )
    local.start()
    local.wait()
    for copy in copies:
        copy.wait_send()
        copy.wait_recv()


def exchange(parts, axis, size, spread, tag):
    shape = (size,) + parts.shape[1 - spread:]
    nbytes = math.prod(shape) * parts.dtype.itemsize
    return pl.pallas_call(
        functools.partial(exchange_kernel, axis, size, spread),
        out_shape=jax.ShapeDtypeStruct(shape, parts.dtype),
        in_specs=[pl.BlockSpec(memory_space=pl.ANY)],
        out_specs=pl.BlockSpec(memory_space=pl.ANY),
        scratch_shapes=[
            pltpu.SemaphoreType.DMA,
            pltpu.SemaphoreType.DMA((size,)),
            pltpu.SemaphoreType.DMA((size,)),
        ],
        compiler_params=pltpu.CompilerParams(collective_id=tag, has_side_effects=True),
        cost_estimate=pl.CostEstimate(flops=0, transcendentals=0, bytes_accessed=2 * nbytes),
    )(parts)


def gather_all(value, axis, size):
    spread = jnp.broadcast_to(value[None], (size,) + value.shape)
    got = lax.all_to_all(spread, axis, 0, 0, tiled=False)
    return got.reshape((size * value.shape[0],) + value.shape[1:])


def scatter_sum_native(value, axis, size):
    parts = value.reshape((size, value.shape[0] // size) + value.shape[1:])
    got = lax.all_to_all(parts, axis, 0, 0, tiled=False)
    return jnp.sum(got.astype(jnp.float32), axis=0)


def scatter_sum(value, axis, size, tag):
    parts = value.reshape((size, value.shape[0] // size) + value.shape[1:])
    got = exchange(parts, axis, size, False, tag)
    return jnp.sum(got.astype(jnp.float32), axis=0)


def per_device(features, weight, bias, cotangent, tiles, tile_rows, tile_cols, tile_counts):
    tile_set = tiles[0, 0]
    dest_ids = tile_rows[0, 0]
    source_ids = tile_cols[0, 0]
    live_count = tile_counts[0, 0]
    block = tile_set.shape[-1]
    own_nodes = features.shape[0]
    width = features.shape[1]
    row_count = lax.axis_size("row")
    col_count = lax.axis_size("col")
    blocks_down = own_nodes * col_count // block
    blocks_across = own_nodes * row_count // block
    factor = 1.0 / math.sqrt(own_nodes * row_count * col_count)
    panel = gather_all(features, "row", row_count)
    panel_blocks = panel.reshape(blocks_across, block, width)
    partial_value = accumulate(
        tile_set, dest_ids, source_ids, live_count, panel_blocks, blocks_down, False
    )
    term = partial_value.reshape(blocks_down * block, width)
    summed = scatter_sum_native(term.astype(jnp.bfloat16), "col", col_count)
    aggregated = summed.astype(jnp.bfloat16)
    preact = jnp.dot(aggregated, weight, preferred_element_type=jnp.float32) + bias
    hidden = jax.nn.silu(preact).astype(jnp.bfloat16)
    sigma = jax.nn.sigmoid(preact)
    slope = sigma * (1.0 + preact * (1.0 - sigma))
    grad_pre = (cotangent.astype(jnp.float32) * slope).astype(jnp.bfloat16)
    local_weight = jnp.einsum("nf,ng->fg", aggregated, grad_pre, preferred_element_type=jnp.float32)
    local_bias = jnp.sum(grad_pre.astype(jnp.float32), axis=0)
    grad_agg = jnp.dot(grad_pre, weight.T, preferred_element_type=jnp.float32).astype(jnp.bfloat16)
    packed = jnp.concatenate([local_weight, local_bias[None, :]], axis=0)
    grad_panel = lax.all_gather(grad_agg, "col", axis=0, tiled=True)
    packed = butterfly_sum(packed, (("col", col_count), ("row", row_count)), 1)
    grad_panel, packed = lax.optimization_barrier((grad_panel, packed))
    grad_blocks = grad_panel.reshape(blocks_down, block, width)
    partial_back = accumulate(
        tile_set, dest_ids, source_ids, live_count, grad_blocks, blocks_across, True
    )
    term_back = partial_back.reshape(blocks_across * block, width)
    grad_features = scatter_sum(term_back.astype(jnp.bfloat16), "row", row_count, 0).astype(
        jnp.bfloat16
    )
    grad_weight = packed[:width] * factor
    grad_bias = packed[width] * factor
    return (hidden, grad_weight, grad_bias, grad_features)


def solution(mesh):
    in_specs = (
        P(("col", "row"), None),
        P(),
        P(),
        P(("row", "col"), None),
        P("row", "col", None, None, None),
        P("row", "col", None),
        P("row", "col", None),
        P("row", "col"),
    )
    out_specs = (P(("row", "col"), None), P(), P(), P(("col", "row"), None))
    return jax.shard_map(
        per_device, mesh=mesh, in_specs=in_specs, out_specs=out_specs, check_vma=False
    )
```

```python
import functools
import math

import jax
import jax.numpy as jnp
from jax import lax
from jax.experimental import pallas as pl
from jax.experimental.pallas import tpu as pltpu
from jax.sharding import PartitionSpec as P

GROUP = 32
UNROLL = 32


def accumulate_kernel(backward, dest_ref, source_ref, count_ref, tiles_ref, panel_ref, out_ref):
    step = pl.program_id(0)
    group = tiles_ref.shape[0]
    out_blocks = out_ref.shape[0]
    in_blocks = panel_ref.shape[0]

    @pl.when(step == 0)
    def _():
        out_ref[...] = jnp.zeros_like(out_ref)

    base = step * group
    live_count = count_ref[0]

    def one_tile(i, checked):
        slot = base + i
        if backward:
            fetch = jnp.clip(dest_ref[slot], 0, in_blocks - 1)
            target = jnp.clip(source_ref[slot], 0, out_blocks - 1)
            contrib = lax.dot_general(
                tiles_ref[i], panel_ref[fetch], (((0,), (0,)), ((), ())),
                preferred_element_type=jnp.float32,
            )
        else:
            fetch = jnp.clip(source_ref[slot], 0, in_blocks - 1)
            target = jnp.clip(dest_ref[slot], 0, out_blocks - 1)
            contrib = jnp.dot(
                tiles_ref[i], panel_ref[fetch], preferred_element_type=jnp.float32
            )
        if checked:
            contrib = jnp.where(slot < live_count, contrib, 0.0)
        out_ref[target] += contrib

    @pl.when(base + group <= live_count)
    def _():
        @pl.loop(0, group, unroll=UNROLL)
        def _(i):
            one_tile(i, False)

    @pl.when((base < live_count) & (base + group > live_count))
    def _():
        @pl.loop(0, group)
        def _(i):
            one_tile(i, True)


def accumulate(tiles, dest_ids, source_ids, live_count, source_blocks, out_blocks, backward):
    slots, block, _ = tiles.shape
    width = source_blocks.shape[-1]
    in_blocks = source_blocks.shape[0]
    group = math.gcd(slots, GROUP)
    steps = slots // group

    def tile_map(g, dest, source, count):
        last = jnp.maximum(count[0] - 1, 0) // group
        return (jnp.minimum(g, last), 0, 0)

    flops = 2 * slots * block * block * width
    bytes_accessed = tiles.size * 2 + source_blocks.size * 2 + out_blocks * block * width * 4
    return pl.pallas_call(
        functools.partial(accumulate_kernel, backward),
        out_shape=jax.ShapeDtypeStruct((out_blocks, block, width), jnp.float32),
        grid_spec=pltpu.PrefetchScalarGridSpec(
            num_scalar_prefetch=3,
            grid=(steps,),
            in_specs=[
                pl.BlockSpec((group, block, block), tile_map),
                pl.BlockSpec((in_blocks, block, width), lambda g, d, s, c: (0, 0, 0)),
            ],
            out_specs=pl.BlockSpec((out_blocks, block, width), lambda g, d, s, c: (0, 0, 0)),
        ),
        compiler_params=pltpu.CompilerParams(
            dimension_semantics=("arbitrary",), vmem_limit_bytes=60 * 1024 * 1024
        ),
        cost_estimate=pl.CostEstimate(
            flops=flops, transcendentals=0, bytes_accessed=bytes_accessed
        ),
    )(dest_ids, source_ids, live_count.reshape(1), tiles, source_blocks)


def butterfly_kernel(steps, value_ref, out_ref, slots, send_sems, recv_sems):
    partners = []
    for axis, distance in steps:
        me = lax.axis_index(axis)
        bit = (me // distance) % 2
        partners.append((axis, me + distance - 2 * distance * bit))
    barrier = pltpu.get_barrier_semaphore()
    for axis, partner in partners:
        pl.semaphore_signal(
            barrier, 1, device_id={axis: partner}, device_id_type=pl.DeviceIdType.MESH
        )
    pl.semaphore_wait(barrier, len(partners))
    out_ref[...] = value_ref[...]
    for index, (axis, partner) in enumerate(partners):
        copy = pltpu.make_async_remote_copy(
            src_ref=out_ref,
            dst_ref=slots.at[index],
            send_sem=send_sems.at[index],
            recv_sem=recv_sems.at[index],
            device_id={axis: partner},
            device_id_type=pl.DeviceIdType.MESH,
        )
        copy.start()
        copy.wait_send()
        copy.wait_recv()
        out_ref[...] = out_ref[...] + slots[index]


def butterfly_sum(value, axes, tag):
    steps = []
    for axis, size in axes:
        distance = 1
        while distance < size:
            steps.append((axis, distance))
            distance *= 2
    count = len(steps)
    return pl.pallas_call(
        functools.partial(butterfly_kernel, tuple(steps)),
        out_shape=jax.ShapeDtypeStruct(value.shape, value.dtype),
        in_specs=[pl.BlockSpec(memory_space=pltpu.VMEM)],
        out_specs=pl.BlockSpec(memory_space=pltpu.VMEM),
        scratch_shapes=[
            pltpu.VMEM((count,) + value.shape, value.dtype),
            pltpu.SemaphoreType.DMA((count,)),
            pltpu.SemaphoreType.DMA((count,)),
        ],
        compiler_params=pltpu.CompilerParams(collective_id=tag, has_side_effects=True),
    )(value)


def exchange_kernel(axis, size, spread, parts_ref, value_ref, out_ref, sum_ref, local_sem,
                    send_sems, recv_sems, slots, sum_send_sems, sum_recv_sems):
    me = lax.axis_index(axis)
    barrier = pltpu.get_barrier_semaphore()
    for shift in range(1, size):
        pl.semaphore_signal(
            barrier, 1, device_id={axis: lax.rem(me + shift, size)},
            device_id_type=pl.DeviceIdType.MESH,
        )
    pl.semaphore_wait(barrier, size - 1)
    copies = []
    for shift in range(1, size):
        peer = lax.rem(me + shift, size)
        copy = pltpu.make_async_remote_copy(
            src_ref=parts_ref if spread else parts_ref.at[peer],
            dst_ref=out_ref.at[me],
            send_sem=send_sems.at[shift],
            recv_sem=recv_sems.at[shift],
            device_id={axis: peer},
            device_id_type=pl.DeviceIdType.MESH,
        )
        copy.start()
        copies.append(copy)
    local = pltpu.make_async_copy(
        parts_ref if spread else parts_ref.at[me], out_ref.at[me], local_sem
    )
    local.start()
    sum_ref[...] = value_ref[...]
    distance = 1
    index = 0
    while distance < size:
        bit = (me // distance) % 2
        partner = me + distance - 2 * distance * bit
        step = pltpu.make_async_remote_copy(
            src_ref=sum_ref,
            dst_ref=slots.at[index],
            send_sem=sum_send_sems.at[index],
            recv_sem=sum_recv_sems.at[index],
            device_id={axis: partner},
            device_id_type=pl.DeviceIdType.MESH,
        )
        step.start()
        step.wait_send()
        step.wait_recv()
        sum_ref[...] = sum_ref[...] + slots[index]
        distance *= 2
        index += 1
    local.wait()
    for copy in copies:
        copy.wait_send()
        copy.wait_recv()


def exchange(parts, value, axis, size, spread, tag):
    shape = (size,) + parts.shape[1 - spread:]
    nbytes = math.prod(shape) * parts.dtype.itemsize
    steps = max(size.bit_length() - 1, 1)
    return pl.pallas_call(
        functools.partial(exchange_kernel, axis, size, spread),
        out_shape=(
            jax.ShapeDtypeStruct(shape, parts.dtype),
            jax.ShapeDtypeStruct(value.shape, value.dtype),
        ),
        in_specs=[pl.BlockSpec(memory_space=pl.ANY), pl.BlockSpec(memory_space=pltpu.VMEM)],
        out_specs=(pl.BlockSpec(memory_space=pl.ANY), pl.BlockSpec(memory_space=pltpu.VMEM)),
        scratch_shapes=[
            pltpu.SemaphoreType.DMA,
            pltpu.SemaphoreType.DMA((size,)),
            pltpu.SemaphoreType.DMA((size,)),
            pltpu.VMEM((steps,) + value.shape, value.dtype),
            pltpu.SemaphoreType.DMA((steps,)),
            pltpu.SemaphoreType.DMA((steps,)),
        ],
        compiler_params=pltpu.CompilerParams(collective_id=tag, has_side_effects=True),
        cost_estimate=pl.CostEstimate(flops=0, transcendentals=0, bytes_accessed=2 * nbytes),
    )(parts, value)


def gather_all(value, axis, size):
    spread = jnp.broadcast_to(value[None], (size,) + value.shape)
    got = lax.all_to_all(spread, axis, 0, 0, tiled=False)
    return got.reshape((size * value.shape[0],) + value.shape[1:])


def scatter_sum_native(value, axis, size):
    parts = value.reshape((size, value.shape[0] // size) + value.shape[1:])
    got = lax.all_to_all(parts, axis, 0, 0, tiled=False)
    return jnp.sum(got.astype(jnp.float32), axis=0)


def scatter_sum(value, extra, axis, size, tag):
    parts = value.reshape((size, value.shape[0] // size) + value.shape[1:])
    got, extra = exchange(parts, extra, axis, size, False, tag)
    return jnp.sum(got.astype(jnp.float32), axis=0), extra


def per_device(features, weight, bias, cotangent, tiles, tile_rows, tile_cols, tile_counts):
    tile_set = tiles[0, 0]
    dest_ids = tile_rows[0, 0]
    source_ids = tile_cols[0, 0]
    live_count = tile_counts[0, 0]
    block = tile_set.shape[-1]
    own_nodes = features.shape[0]
    width = features.shape[1]
    row_count = lax.axis_size("row")
    col_count = lax.axis_size("col")
    blocks_down = own_nodes * col_count // block
    blocks_across = own_nodes * row_count // block
    factor = 1.0 / math.sqrt(own_nodes * row_count * col_count)
    panel = gather_all(features, "row", row_count)
    panel_blocks = panel.reshape(blocks_across, block, width)
    partial_value = accumulate(
        tile_set, dest_ids, source_ids, live_count, panel_blocks, blocks_down, False
    )
    term = partial_value.reshape(blocks_down * block, width)
    summed = scatter_sum_native(term.astype(jnp.bfloat16), "col", col_count)
    aggregated = summed.astype(jnp.bfloat16)
    preact = jnp.dot(aggregated, weight, preferred_element_type=jnp.float32) + bias
    hidden = jax.nn.silu(preact).astype(jnp.bfloat16)
    sigma = jax.nn.sigmoid(preact)
    slope = sigma * (1.0 + preact * (1.0 - sigma))
    grad_pre = (cotangent.astype(jnp.float32) * slope).astype(jnp.bfloat16)
    local_weight = jnp.einsum("nf,ng->fg", aggregated, grad_pre, preferred_element_type=jnp.float32)
    local_bias = jnp.sum(grad_pre.astype(jnp.float32), axis=0)
    grad_agg = jnp.dot(grad_pre, weight.T, preferred_element_type=jnp.float32).astype(jnp.bfloat16)
    packed = jnp.concatenate([local_weight, local_bias[None, :]], axis=0)
    grad_panel = lax.all_gather(grad_agg, "col", axis=0, tiled=True)
    packed = butterfly_sum(packed, (("col", col_count),), 1)
    grad_panel, packed = lax.optimization_barrier((grad_panel, packed))
    grad_blocks = grad_panel.reshape(blocks_down, block, width)
    partial_back = accumulate(
        tile_set, dest_ids, source_ids, live_count, grad_blocks, blocks_across, True
    )
    term_back = partial_back.reshape(blocks_across * block, width)
    grad_features, packed = scatter_sum(
        term_back.astype(jnp.bfloat16), packed, "row", row_count, 0
    )
    grad_features = grad_features.astype(jnp.bfloat16)
    grad_weight = packed[:width] * factor
    grad_bias = packed[width] * factor
    return (hidden, grad_weight, grad_bias, grad_features)


def solution(mesh):
    in_specs = (
        P(("col", "row"), None),
        P(),
        P(),
        P(("row", "col"), None),
        P("row", "col", None, None, None),
        P("row", "col", None),
        P("row", "col", None),
        P("row", "col"),
    )
    out_specs = (P(("row", "col"), None), P(), P(), P(("col", "row"), None))
    return jax.shard_map(
        per_device, mesh=mesh, in_specs=in_specs, out_specs=out_specs, check_vma=False
    )
```

```python
import functools
import math

import jax
import jax.numpy as jnp
from jax import lax
from jax.experimental import pallas as pl
from jax.experimental.pallas import tpu as pltpu
from jax.sharding import PartitionSpec as P

GROUP = 32
UNROLL = 32


def accumulate_kernel(backward, dest_ref, source_ref, count_ref, tiles_ref, panel_ref, out_ref):
    step = pl.program_id(0)
    group = tiles_ref.shape[0]
    out_blocks = out_ref.shape[0]
    in_blocks = panel_ref.shape[0]

    @pl.when(step == 0)
    def _():
        out_ref[...] = jnp.zeros_like(out_ref)

    base = step * group
    live_count = count_ref[0]

    def one_tile(i, checked):
        slot = base + i
        if backward:
            fetch = jnp.clip(dest_ref[slot], 0, in_blocks - 1)
            target = jnp.clip(source_ref[slot], 0, out_blocks - 1)
            contrib = lax.dot_general(
                tiles_ref[i], panel_ref[fetch], (((0,), (0,)), ((), ())),
                preferred_element_type=jnp.float32,
            )
        else:
            fetch = jnp.clip(source_ref[slot], 0, in_blocks - 1)
            target = jnp.clip(dest_ref[slot], 0, out_blocks - 1)
            contrib = jnp.dot(
                tiles_ref[i], panel_ref[fetch], preferred_element_type=jnp.float32
            )
        if checked:
            contrib = jnp.where(slot < live_count, contrib, 0.0)
        out_ref[target] += contrib

    @pl.when(base + group <= live_count)
    def _():
        @pl.loop(0, group, unroll=UNROLL)
        def _(i):
            one_tile(i, False)

    @pl.when((base < live_count) & (base + group > live_count))
    def _():
        @pl.loop(0, group)
        def _(i):
            one_tile(i, True)


def accumulate(tiles, dest_ids, source_ids, live_count, source_blocks, out_blocks, backward):
    slots, block, _ = tiles.shape
    width = source_blocks.shape[-1]
    in_blocks = source_blocks.shape[0]
    group = math.gcd(slots, GROUP)
    steps = slots // group

    def tile_map(g, dest, source, count):
        last = jnp.maximum(count[0] - 1, 0) // group
        return (jnp.minimum(g, last), 0, 0)

    flops = 2 * slots * block * block * width
    bytes_accessed = tiles.size * 2 + source_blocks.size * 2 + out_blocks * block * width * 4
    return pl.pallas_call(
        functools.partial(accumulate_kernel, backward),
        out_shape=jax.ShapeDtypeStruct((out_blocks, block, width), jnp.float32),
        grid_spec=pltpu.PrefetchScalarGridSpec(
            num_scalar_prefetch=3,
            grid=(steps,),
            in_specs=[
                pl.BlockSpec((group, block, block), tile_map),
                pl.BlockSpec((in_blocks, block, width), lambda g, d, s, c: (0, 0, 0)),
            ],
            out_specs=pl.BlockSpec((out_blocks, block, width), lambda g, d, s, c: (0, 0, 0)),
        ),
        compiler_params=pltpu.CompilerParams(
            dimension_semantics=("arbitrary",), vmem_limit_bytes=60 * 1024 * 1024
        ),
        cost_estimate=pl.CostEstimate(
            flops=flops, transcendentals=0, bytes_accessed=bytes_accessed
        ),
    )(dest_ids, source_ids, live_count.reshape(1), tiles, source_blocks)


def butterfly_kernel(steps, value_ref, out_ref, slots, send_sems, recv_sems):
    partners = []
    for axis, distance in steps:
        me = lax.axis_index(axis)
        bit = (me // distance) % 2
        partners.append((axis, me + distance - 2 * distance * bit))
    barrier = pltpu.get_barrier_semaphore()
    for axis, partner in partners:
        pl.semaphore_signal(
            barrier, 1, device_id={axis: partner}, device_id_type=pl.DeviceIdType.MESH
        )
    pl.semaphore_wait(barrier, len(partners))
    out_ref[...] = value_ref[...]
    for index, (axis, partner) in enumerate(partners):
        copy = pltpu.make_async_remote_copy(
            src_ref=out_ref,
            dst_ref=slots.at[index],
            send_sem=send_sems.at[index],
            recv_sem=recv_sems.at[index],
            device_id={axis: partner},
            device_id_type=pl.DeviceIdType.MESH,
        )
        copy.start()
        copy.wait_send()
        copy.wait_recv()
        out_ref[...] = out_ref[...] + slots[index]


def butterfly_sum(value, axes, tag):
    steps = []
    for axis, size in axes:
        distance = 1
        while distance < size:
            steps.append((axis, distance))
            distance *= 2
    count = len(steps)
    return pl.pallas_call(
        functools.partial(butterfly_kernel, tuple(steps)),
        out_shape=jax.ShapeDtypeStruct(value.shape, value.dtype),
        in_specs=[pl.BlockSpec(memory_space=pltpu.VMEM)],
        out_specs=pl.BlockSpec(memory_space=pltpu.VMEM),
        scratch_shapes=[
            pltpu.VMEM((count,) + value.shape, value.dtype),
            pltpu.SemaphoreType.DMA((count,)),
            pltpu.SemaphoreType.DMA((count,)),
        ],
        compiler_params=pltpu.CompilerParams(collective_id=tag, has_side_effects=True),
    )(value)


def exchange_kernel(axis, size, spread, parts_ref, out_ref, local_sem, send_sems, recv_sems):
    me = lax.axis_index(axis)
    barrier = pltpu.get_barrier_semaphore()
    for shift in range(1, size):
        pl.semaphore_signal(
            barrier, 1, device_id={axis: lax.rem(me + shift, size)},
            device_id_type=pl.DeviceIdType.MESH,
        )
    pl.semaphore_wait(barrier, size - 1)
    copies = []
    for shift in range(1, size):
        peer = lax.rem(me + shift, size)
        copy = pltpu.make_async_remote_copy(
            src_ref=parts_ref if spread else parts_ref.at[peer],
            dst_ref=out_ref.at[me],
            send_sem=send_sems.at[shift],
            recv_sem=recv_sems.at[shift],
            device_id={axis: peer},
            device_id_type=pl.DeviceIdType.MESH,
        )
        copy.start()
        copies.append(copy)
    local = pltpu.make_async_copy(
        parts_ref if spread else parts_ref.at[me], out_ref.at[me], local_sem
    )
    local.start()
    local.wait()
    for copy in copies:
        copy.wait_send()
        copy.wait_recv()


def exchange(parts, axis, size, spread, tag):
    shape = (size,) + parts.shape[1 - spread:]
    nbytes = math.prod(shape) * parts.dtype.itemsize
    return pl.pallas_call(
        functools.partial(exchange_kernel, axis, size, spread),
        out_shape=jax.ShapeDtypeStruct(shape, parts.dtype),
        in_specs=[pl.BlockSpec(memory_space=pl.ANY)],
        out_specs=pl.BlockSpec(memory_space=pl.ANY),
        scratch_shapes=[
            pltpu.SemaphoreType.DMA,
            pltpu.SemaphoreType.DMA((size,)),
            pltpu.SemaphoreType.DMA((size,)),
        ],
        compiler_params=pltpu.CompilerParams(collective_id=tag, has_side_effects=True),
        cost_estimate=pl.CostEstimate(flops=0, transcendentals=0, bytes_accessed=2 * nbytes),
    )(parts)


def gather_all(value, axis, size):
    spread = jnp.broadcast_to(value[None], (size,) + value.shape)
    got = lax.all_to_all(spread, axis, 0, 0, tiled=False)
    return got.reshape((size * value.shape[0],) + value.shape[1:])


def scatter_sum_native(value, axis, size):
    parts = value.reshape((size, value.shape[0] // size) + value.shape[1:])
    got = lax.all_to_all(parts, axis, 0, 0, tiled=False)
    return jnp.sum(got.astype(jnp.float32), axis=0)


def scatter_sum(value, axis, size, tag):
    parts = value.reshape((size, value.shape[0] // size) + value.shape[1:])
    got = exchange(parts, axis, size, False, tag)
    return jnp.sum(got.astype(jnp.float32), axis=0)


def per_device(features, weight, bias, cotangent, tiles, tile_rows, tile_cols, tile_counts):
    tile_set = tiles[0, 0]
    dest_ids = tile_rows[0, 0]
    source_ids = tile_cols[0, 0]
    live_count = tile_counts[0, 0]
    block = tile_set.shape[-1]
    own_nodes = features.shape[0]
    width = features.shape[1]
    row_count = lax.axis_size("row")
    col_count = lax.axis_size("col")
    blocks_down = own_nodes * col_count // block
    blocks_across = own_nodes * row_count // block
    factor = 1.0 / math.sqrt(own_nodes * row_count * col_count)
    panel = gather_all(features, "row", row_count)
    panel_blocks = panel.reshape(blocks_across, block, width)
    partial_value = accumulate(
        tile_set, dest_ids, source_ids, live_count, panel_blocks, blocks_down, False
    )
    term = partial_value.reshape(blocks_down * block, width)
    summed = scatter_sum_native(term.astype(jnp.bfloat16), "col", col_count)
    aggregated = summed.astype(jnp.bfloat16)
    preact = jnp.dot(aggregated, weight, preferred_element_type=jnp.float32) + bias
    hidden = jax.nn.silu(preact).astype(jnp.bfloat16)
    sigma = jax.nn.sigmoid(preact)
    slope = sigma * (1.0 + preact * (1.0 - sigma))
    grad_pre = (cotangent.astype(jnp.float32) * slope).astype(jnp.bfloat16)
    local_weight = jnp.einsum("nf,ng->fg", aggregated, grad_pre, preferred_element_type=jnp.float32)
    local_bias = jnp.sum(grad_pre.astype(jnp.float32), axis=0)
    grad_agg = jnp.dot(grad_pre, weight.T, preferred_element_type=jnp.float32).astype(jnp.bfloat16)
    packed = jnp.concatenate([local_weight, local_bias[None, :]], axis=0)
    grad_panel = lax.all_gather(grad_agg, "col", axis=0, tiled=True)
    packed = butterfly_sum(packed, (("col", col_count),), 1)
    grad_panel, packed = lax.optimization_barrier((grad_panel, packed))
    grad_blocks = grad_panel.reshape(blocks_down, block, width)
    partial_back = accumulate(
        tile_set, dest_ids, source_ids, live_count, grad_blocks, blocks_across, True
    )
    term_back = partial_back.reshape(blocks_across * block, width)
    packed = lax.psum(packed, "row")
    grad_features = scatter_sum(term_back.astype(jnp.bfloat16), "row", row_count, 0).astype(
        jnp.bfloat16
    )
    grad_weight = packed[:width] * factor
    grad_bias = packed[width] * factor
    return (hidden, grad_weight, grad_bias, grad_features)


def solution(mesh):
    in_specs = (
        P(("col", "row"), None),
        P(),
        P(),
        P(("row", "col"), None),
        P("row", "col", None, None, None),
        P("row", "col", None),
        P("row", "col", None),
        P("row", "col"),
    )
    out_specs = (P(("row", "col"), None), P(), P(), P(("col", "row"), None))
    return jax.shard_map(
        per_device, mesh=mesh, in_specs=in_specs, out_specs=out_specs, check_vma=False
    )
```

```python
import functools
import math

import jax
import jax.numpy as jnp
from jax import lax
from jax.experimental import pallas as pl
from jax.experimental.pallas import tpu as pltpu
from jax.sharding import PartitionSpec as P

GROUP = 128
UNROLL = 128


def accumulate_kernel(backward, dest_ref, source_ref, count_ref, tiles_ref, panel_ref, out_ref):
    step = pl.program_id(0)
    group = tiles_ref.shape[0]
    out_blocks = out_ref.shape[0]
    in_blocks = panel_ref.shape[0]

    @pl.when(step == 0)
    def _():
        out_ref[...] = jnp.zeros_like(out_ref)

    base = step * group
    live_count = count_ref[0]

    def one_tile(i, checked):
        slot = base + i
        if backward:
            fetch = jnp.clip(dest_ref[slot], 0, in_blocks - 1)
            target = jnp.clip(source_ref[slot], 0, out_blocks - 1)
            contrib = lax.dot_general(
                tiles_ref[i], panel_ref[fetch], (((0,), (0,)), ((), ())),
                preferred_element_type=jnp.float32,
            )
        else:
            fetch = jnp.clip(source_ref[slot], 0, in_blocks - 1)
            target = jnp.clip(dest_ref[slot], 0, out_blocks - 1)
            contrib = jnp.dot(
                tiles_ref[i], panel_ref[fetch], preferred_element_type=jnp.float32
            )
        if checked:
            contrib = jnp.where(slot < live_count, contrib, 0.0)
        out_ref[target] += contrib

    @pl.when(base + group <= live_count)
    def _():
        @pl.loop(0, group, unroll=UNROLL)
        def _(i):
            one_tile(i, False)

    @pl.when((base < live_count) & (base + group > live_count))
    def _():
        @pl.loop(0, group)
        def _(i):
            one_tile(i, True)


def accumulate(tiles, dest_ids, source_ids, live_count, source_blocks, out_blocks, backward):
    slots, block, _ = tiles.shape
    width = source_blocks.shape[-1]
    in_blocks = source_blocks.shape[0]
    group = math.gcd(slots, GROUP)
    steps = slots // group

    def tile_map(g, dest, source, count):
        last = jnp.maximum(count[0] - 1, 0) // group
        return (jnp.minimum(g, last), 0, 0)

    flops = 2 * slots * block * block * width
    bytes_accessed = tiles.size * 2 + source_blocks.size * 2 + out_blocks * block * width * 4
    return pl.pallas_call(
        functools.partial(accumulate_kernel, backward),
        out_shape=jax.ShapeDtypeStruct((out_blocks, block, width), jnp.float32),
        grid_spec=pltpu.PrefetchScalarGridSpec(
            num_scalar_prefetch=3,
            grid=(steps,),
            in_specs=[
                pl.BlockSpec((group, block, block), tile_map),
                pl.BlockSpec((in_blocks, block, width), lambda g, d, s, c: (0, 0, 0)),
            ],
            out_specs=pl.BlockSpec((out_blocks, block, width), lambda g, d, s, c: (0, 0, 0)),
        ),
        compiler_params=pltpu.CompilerParams(
            dimension_semantics=("arbitrary",), vmem_limit_bytes=60 * 1024 * 1024
        ),
        cost_estimate=pl.CostEstimate(
            flops=flops, transcendentals=0, bytes_accessed=bytes_accessed
        ),
    )(dest_ids, source_ids, live_count.reshape(1), tiles, source_blocks)


def butterfly_sum(value, axis):
    size = lax.axis_size(axis)
    distance = 1
    while distance < size:
        pairs = [(i, i ^ distance) for i in range(size)]
        value = value + lax.ppermute(value, axis, pairs)
        distance *= 2
    return value


def gather_all(value, axis, size):
    spread = jnp.broadcast_to(value[None], (size,) + value.shape)
    got = lax.all_to_all(spread, axis, 0, 0, tiled=False)
    return got.reshape((size * value.shape[0],) + value.shape[1:])


def scatter_sum(value, axis, size):
    parts = value.reshape((size, value.shape[0] // size) + value.shape[1:])
    got = lax.all_to_all(parts, axis, 0, 0, tiled=False)
    return jnp.sum(got.astype(jnp.float32), axis=0)


def per_device(features, weight, bias, cotangent, tiles, tile_rows, tile_cols, tile_counts):
    tile_set = tiles[0, 0]
    dest_ids = tile_rows[0, 0]
    source_ids = tile_cols[0, 0]
    live_count = tile_counts[0, 0]
    block = tile_set.shape[-1]
    own_nodes = features.shape[0]
    width = features.shape[1]
    row_count = lax.axis_size("row")
    col_count = lax.axis_size("col")
    blocks_down = own_nodes * col_count // block
    blocks_across = own_nodes * row_count // block
    factor = 1.0 / math.sqrt(own_nodes * row_count * col_count)
    panel = gather_all(features, "row", row_count)
    panel_blocks = panel.reshape(blocks_across, block, width)
    partial_value = accumulate(
        tile_set, dest_ids, source_ids, live_count, panel_blocks, blocks_down, False
    )
    term = partial_value.reshape(blocks_down * block, width)
    summed = scatter_sum(term.astype(jnp.bfloat16), "col", col_count)
    aggregated = summed.astype(jnp.bfloat16)
    preact = jnp.dot(aggregated, weight, preferred_element_type=jnp.float32) + bias
    hidden = jax.nn.silu(preact).astype(jnp.bfloat16)
    sigma = jax.nn.sigmoid(preact)
    slope = sigma * (1.0 + preact * (1.0 - sigma))
    grad_pre = (cotangent.astype(jnp.float32) * slope).astype(jnp.bfloat16)
    local_weight = jnp.einsum("nf,ng->fg", aggregated, grad_pre, preferred_element_type=jnp.float32)
    local_bias = jnp.sum(grad_pre.astype(jnp.float32), axis=0)
    grad_agg = jnp.dot(grad_pre, weight.T, preferred_element_type=jnp.float32).astype(jnp.bfloat16)
    packed = jnp.concatenate([local_weight, local_bias[None, :]], axis=0)
    grad_panel = lax.all_gather(grad_agg, "col", axis=0, tiled=True)
    packed = butterfly_sum(butterfly_sum(packed, "col"), "row")
    grad_panel, packed = lax.optimization_barrier((grad_panel, packed))
    grad_blocks = grad_panel.reshape(blocks_down, block, width)
    partial_back = accumulate(
        tile_set, dest_ids, source_ids, live_count, grad_blocks, blocks_across, True
    )
    term_back = partial_back.reshape(blocks_across * block, width)
    grad_features = scatter_sum(term_back.astype(jnp.bfloat16), "row", row_count).astype(
        jnp.bfloat16
    )
    grad_weight = packed[:width] * factor
    grad_bias = packed[width] * factor
    return (hidden, grad_weight, grad_bias, grad_features)


def solution(mesh):
    in_specs = (
        P(("col", "row"), None),
        P(),
        P(),
        P(("row", "col"), None),
        P("row", "col", None, None, None),
        P("row", "col", None),
        P("row", "col", None),
        P("row", "col"),
    )
    out_specs = (P(("row", "col"), None), P(), P(), P(("col", "row"), None))
    return jax.shard_map(
        per_device, mesh=mesh, in_specs=in_specs, out_specs=out_specs, check_vma=False
    )
```

```python
import functools
import math

import jax
import jax.numpy as jnp
from jax import lax
from jax.experimental import pallas as pl
from jax.experimental.pallas import tpu as pltpu
from jax.sharding import PartitionSpec as P

GROUP = 64
UNROLL = 64


def accumulate_kernel(backward, dest_ref, source_ref, count_ref, tiles_ref, panel_ref, out_ref):
    step = pl.program_id(0)
    group = tiles_ref.shape[0]
    out_blocks = out_ref.shape[0]
    in_blocks = panel_ref.shape[0]

    @pl.when(step == 0)
    def _():
        out_ref[...] = jnp.zeros_like(out_ref)

    base = step * group
    live_count = count_ref[0]

    def one_tile(i, checked):
        slot = base + i
        tile = tiles_ref[i]
        if checked:
            tile = jnp.where(slot < live_count, tile, jnp.zeros_like(tile))
        if backward:
            fetch = jnp.clip(dest_ref[slot], 0, in_blocks - 1)
            target = jnp.clip(source_ref[slot], 0, out_blocks - 1)
            contrib = lax.dot_general(
                tile, panel_ref[fetch], (((0,), (0,)), ((), ())),
                preferred_element_type=jnp.float32,
            )
        else:
            fetch = jnp.clip(source_ref[slot], 0, in_blocks - 1)
            target = jnp.clip(dest_ref[slot], 0, out_blocks - 1)
            contrib = jnp.dot(tile, panel_ref[fetch], preferred_element_type=jnp.float32)
        out_ref[target] += contrib

    @pl.when(base + group <= live_count)
    def _():
        @pl.loop(0, group, unroll=UNROLL)
        def _(i):
            one_tile(i, False)

    @pl.when((base < live_count) & (base + group > live_count))
    def _():
        @pl.loop(0, group, unroll=UNROLL)
        def _(i):
            one_tile(i, True)


def accumulate(tiles, dest_ids, source_ids, live_count, source_blocks, out_blocks, backward):
    slots, block, _ = tiles.shape
    width = source_blocks.shape[-1]
    in_blocks = source_blocks.shape[0]
    group = math.gcd(slots, GROUP)
    steps = slots // group

    def tile_map(g, dest, source, count):
        last = jnp.maximum(count[0] - 1, 0) // group
        return (jnp.minimum(g, last), 0, 0)

    flops = 2 * slots * block * block * width
    bytes_accessed = tiles.size * 2 + source_blocks.size * 2 + out_blocks * block * width * 4
    return pl.pallas_call(
        functools.partial(accumulate_kernel, backward),
        out_shape=jax.ShapeDtypeStruct((out_blocks, block, width), jnp.float32),
        grid_spec=pltpu.PrefetchScalarGridSpec(
            num_scalar_prefetch=3,
            grid=(steps,),
            in_specs=[
                pl.BlockSpec((group, block, block), tile_map),
                pl.BlockSpec((in_blocks, block, width), lambda g, d, s, c: (0, 0, 0)),
            ],
            out_specs=pl.BlockSpec((out_blocks, block, width), lambda g, d, s, c: (0, 0, 0)),
        ),
        compiler_params=pltpu.CompilerParams(
            dimension_semantics=("arbitrary",), vmem_limit_bytes=60 * 1024 * 1024
        ),
        cost_estimate=pl.CostEstimate(
            flops=flops, transcendentals=0, bytes_accessed=bytes_accessed
        ),
    )(dest_ids, source_ids, live_count.reshape(1), tiles, source_blocks)


def butterfly_sum(value, axis):
    size = lax.axis_size(axis)
    distance = 1
    while distance < size:
        pairs = [(i, i ^ distance) for i in range(size)]
        value = value + lax.ppermute(value, axis, pairs)
        distance *= 2
    return value


def gather_all(value, axis, size):
    spread = jnp.broadcast_to(value[None], (size,) + value.shape)
    got = lax.all_to_all(spread, axis, 0, 0, tiled=False)
    return got.reshape((size * value.shape[0],) + value.shape[1:])


def scatter_sum(value, axis, size):
    parts = value.reshape((size, value.shape[0] // size) + value.shape[1:])
    got = lax.all_to_all(parts, axis, 0, 0, tiled=False)
    return jnp.sum(got.astype(jnp.float32), axis=0)


def per_device(features, weight, bias, cotangent, tiles, tile_rows, tile_cols, tile_counts):
    tile_set = tiles[0, 0]
    dest_ids = tile_rows[0, 0]
    source_ids = tile_cols[0, 0]
    live_count = tile_counts[0, 0]
    block = tile_set.shape[-1]
    own_nodes = features.shape[0]
    width = features.shape[1]
    row_count = lax.axis_size("row")
    col_count = lax.axis_size("col")
    blocks_down = own_nodes * col_count // block
    blocks_across = own_nodes * row_count // block
    factor = 1.0 / math.sqrt(own_nodes * row_count * col_count)
    panel = gather_all(features, "row", row_count)
    panel_blocks = panel.reshape(blocks_across, block, width)
    partial_value = accumulate(
        tile_set, dest_ids, source_ids, live_count, panel_blocks, blocks_down, False
    )
    term = partial_value.reshape(blocks_down * block, width)
    summed = scatter_sum(term.astype(jnp.bfloat16), "col", col_count)
    aggregated = summed.astype(jnp.bfloat16)
    preact = jnp.dot(aggregated, weight, preferred_element_type=jnp.float32) + bias
    hidden = jax.nn.silu(preact).astype(jnp.bfloat16)
    sigma = jax.nn.sigmoid(preact)
    slope = sigma * (1.0 + preact * (1.0 - sigma))
    grad_pre = (cotangent.astype(jnp.float32) * slope).astype(jnp.bfloat16)
    local_weight = jnp.einsum("nf,ng->fg", aggregated, grad_pre, preferred_element_type=jnp.float32)
    local_bias = jnp.sum(grad_pre.astype(jnp.float32), axis=0)
    grad_agg = jnp.dot(grad_pre, weight.T, preferred_element_type=jnp.float32).astype(jnp.bfloat16)
    packed = jnp.concatenate([local_weight, local_bias[None, :]], axis=0)
    grad_panel = lax.all_gather(grad_agg, "col", axis=0, tiled=True)
    packed = butterfly_sum(butterfly_sum(packed, "col"), "row")
    grad_panel, packed = lax.optimization_barrier((grad_panel, packed))
    grad_blocks = grad_panel.reshape(blocks_down, block, width)
    partial_back = accumulate(
        tile_set, dest_ids, source_ids, live_count, grad_blocks, blocks_across, True
    )
    term_back = partial_back.reshape(blocks_across * block, width)
    grad_features = scatter_sum(term_back.astype(jnp.bfloat16), "row", row_count).astype(
        jnp.bfloat16
    )
    grad_weight = packed[:width] * factor
    grad_bias = packed[width] * factor
    return (hidden, grad_weight, grad_bias, grad_features)


def solution(mesh):
    in_specs = (
        P(("col", "row"), None),
        P(),
        P(),
        P(("row", "col"), None),
        P("row", "col", None, None, None),
        P("row", "col", None),
        P("row", "col", None),
        P("row", "col"),
    )
    out_specs = (P(("row", "col"), None), P(), P(), P(("col", "row"), None))
    return jax.shard_map(
        per_device, mesh=mesh, in_specs=in_specs, out_specs=out_specs, check_vma=False
    )
```

```python
import functools
import math

import jax
import jax.numpy as jnp
from jax import lax
from jax.experimental import pallas as pl
from jax.experimental.pallas import tpu as pltpu
from jax.sharding import PartitionSpec as P

GROUP = 64
UNROLL = 64


def accumulate_kernel(backward, dest_ref, source_ref, count_ref, tiles_ref, panel_ref, out_ref):
    step = pl.program_id(0)
    group = tiles_ref.shape[0]
    out_blocks = out_ref.shape[0]
    in_blocks = panel_ref.shape[0]

    @pl.when(step == 0)
    def _():
        out_ref[...] = jnp.zeros_like(out_ref)

    base = step * group
    live_count = count_ref[0]

    def one_tile(i, checked):
        slot = base + i
        tile = tiles_ref[i]
        if checked:
            tile = jnp.where(slot < live_count, tile, jnp.zeros_like(tile))
        if backward:
            fetch = jnp.clip(dest_ref[slot], 0, in_blocks - 1)
            target = jnp.clip(source_ref[slot], 0, out_blocks - 1)
            contrib = lax.dot_general(
                tile, panel_ref[fetch], (((0,), (0,)), ((), ())),
                preferred_element_type=jnp.float32,
            )
        else:
            fetch = jnp.clip(source_ref[slot], 0, in_blocks - 1)
            target = jnp.clip(dest_ref[slot], 0, out_blocks - 1)
            contrib = jnp.dot(tile, panel_ref[fetch], preferred_element_type=jnp.float32)
        out_ref[target] += contrib

    @pl.when(base + group <= live_count)
    def _():
        @pl.loop(0, group, unroll=UNROLL)
        def _(i):
            one_tile(i, False)

    @pl.when((base < live_count) & (base + group > live_count))
    def _():
        @pl.loop(0, group, unroll=UNROLL)
        def _(i):
            one_tile(i, True)


def accumulate(tiles, dest_ids, source_ids, live_count, source_blocks, out_blocks, backward):
    slots, block, _ = tiles.shape
    width = source_blocks.shape[-1]
    in_blocks = source_blocks.shape[0]
    group = math.gcd(slots, GROUP)
    steps = slots // group

    def tile_map(g, dest, source, count):
        last = jnp.maximum(count[0] - 1, 0) // group
        return (jnp.minimum(g, last), 0, 0)

    flops = 2 * slots * block * block * width
    bytes_accessed = tiles.size * 2 + source_blocks.size * 2 + out_blocks * block * width * 4
    return pl.pallas_call(
        functools.partial(accumulate_kernel, backward),
        out_shape=jax.ShapeDtypeStruct((out_blocks, block, width), jnp.float32),
        grid_spec=pltpu.PrefetchScalarGridSpec(
            num_scalar_prefetch=3,
            grid=(steps,),
            in_specs=[
                pl.BlockSpec((group, block, block), tile_map),
                pl.BlockSpec((in_blocks, block, width), lambda g, d, s, c: (0, 0, 0)),
            ],
            out_specs=pl.BlockSpec((out_blocks, block, width), lambda g, d, s, c: (0, 0, 0)),
        ),
        compiler_params=pltpu.CompilerParams(
            dimension_semantics=("arbitrary",), vmem_limit_bytes=60 * 1024 * 1024
        ),
        cost_estimate=pl.CostEstimate(
            flops=flops, transcendentals=0, bytes_accessed=bytes_accessed
        ),
    )(dest_ids, source_ids, live_count.reshape(1), tiles, source_blocks)


def butterfly_kernel(steps, value_ref, out_ref, outgoing, slots, send_sems, recv_sems):
    partners = []
    for axis, distance in steps:
        me = lax.axis_index(axis)
        bit = (me // distance) % 2
        partners.append((axis, me + distance - 2 * distance * bit))
    barrier = pltpu.get_barrier_semaphore()
    for axis, partner in partners:
        pl.semaphore_signal(
            barrier, 1, device_id={axis: partner}, device_id_type=pl.DeviceIdType.MESH
        )
    pl.semaphore_wait(barrier, len(partners))
    out_ref[...] = value_ref[...]
    for index, (axis, partner) in enumerate(partners):
        outgoing[...] = out_ref[...].astype(outgoing.dtype)
        copy = pltpu.make_async_remote_copy(
            src_ref=outgoing,
            dst_ref=slots.at[index],
            send_sem=send_sems.at[index],
            recv_sem=recv_sems.at[index],
            device_id={axis: partner},
            device_id_type=pl.DeviceIdType.MESH,
        )
        copy.start()
        copy.wait_send()
        copy.wait_recv()
        out_ref[...] = outgoing[...].astype(jnp.float32) + slots[index].astype(jnp.float32)


def butterfly_sum(value, axes, tag):
    steps = []
    for axis, size in axes:
        distance = 1
        while distance < size:
            steps.append((axis, distance))
            distance *= 2
    count = len(steps)
    return pl.pallas_call(
        functools.partial(butterfly_kernel, tuple(steps)),
        out_shape=jax.ShapeDtypeStruct(value.shape, value.dtype),
        in_specs=[pl.BlockSpec(memory_space=pltpu.VMEM)],
        out_specs=pl.BlockSpec(memory_space=pltpu.VMEM),
        scratch_shapes=[
            pltpu.VMEM(value.shape, jnp.bfloat16),
            pltpu.VMEM((count,) + value.shape, jnp.bfloat16),
            pltpu.SemaphoreType.DMA((count,)),
            pltpu.SemaphoreType.DMA((count,)),
        ],
        compiler_params=pltpu.CompilerParams(collective_id=tag, has_side_effects=True),
    )(value)


def gather_all(value, axis, size):
    spread = jnp.broadcast_to(value[None], (size,) + value.shape)
    got = lax.all_to_all(spread, axis, 0, 0, tiled=False)
    return got.reshape((size * value.shape[0],) + value.shape[1:])


def scatter_sum(value, axis, size):
    parts = value.reshape((size, value.shape[0] // size) + value.shape[1:])
    got = lax.all_to_all(parts, axis, 0, 0, tiled=False)
    return jnp.sum(got.astype(jnp.float32), axis=0)


def per_device(features, weight, bias, cotangent, tiles, tile_rows, tile_cols, tile_counts):
    tile_set = tiles[0, 0]
    dest_ids = tile_rows[0, 0]
    source_ids = tile_cols[0, 0]
    live_count = tile_counts[0, 0]
    block = tile_set.shape[-1]
    own_nodes = features.shape[0]
    width = features.shape[1]
    row_count = lax.axis_size("row")
    col_count = lax.axis_size("col")
    blocks_down = own_nodes * col_count // block
    blocks_across = own_nodes * row_count // block
    factor = 1.0 / math.sqrt(own_nodes * row_count * col_count)
    panel = gather_all(features, "row", row_count)
    panel_blocks = panel.reshape(blocks_across, block, width)
    partial_value = accumulate(
        tile_set, dest_ids, source_ids, live_count, panel_blocks, blocks_down, False
    )
    term = partial_value.reshape(blocks_down * block, width)
    summed = scatter_sum(term.astype(jnp.bfloat16), "col", col_count)
    aggregated = summed.astype(jnp.bfloat16)
    preact = jnp.dot(aggregated, weight, preferred_element_type=jnp.float32) + bias
    hidden = jax.nn.silu(preact).astype(jnp.bfloat16)
    sigma = jax.nn.sigmoid(preact)
    slope = sigma * (1.0 + preact * (1.0 - sigma))
    grad_pre = (cotangent.astype(jnp.float32) * slope).astype(jnp.bfloat16)
    local_weight = jnp.einsum("nf,ng->fg", aggregated, grad_pre, preferred_element_type=jnp.float32)
    local_bias = jnp.sum(grad_pre.astype(jnp.float32), axis=0)
    grad_agg = jnp.dot(grad_pre, weight.T, preferred_element_type=jnp.float32).astype(jnp.bfloat16)
    packed = jnp.concatenate([local_weight, local_bias[None, :]], axis=0)
    grad_panel = lax.all_gather(grad_agg, "col", axis=0, tiled=True)
    packed = butterfly_sum(packed, (("col", col_count), ("row", row_count)), 1)
    grad_panel, packed = lax.optimization_barrier((grad_panel, packed))
    grad_blocks = grad_panel.reshape(blocks_down, block, width)
    partial_back = accumulate(
        tile_set, dest_ids, source_ids, live_count, grad_blocks, blocks_across, True
    )
    term_back = partial_back.reshape(blocks_across * block, width)
    grad_features = scatter_sum(term_back.astype(jnp.bfloat16), "row", row_count).astype(
        jnp.bfloat16
    )
    grad_weight = packed[:width] * factor
    grad_bias = packed[width] * factor
    return (hidden, grad_weight, grad_bias, grad_features)


def solution(mesh):
    in_specs = (
        P(("col", "row"), None),
        P(),
        P(),
        P(("row", "col"), None),
        P("row", "col", None, None, None),
        P("row", "col", None),
        P("row", "col", None),
        P("row", "col"),
    )
    out_specs = (P(("row", "col"), None), P(), P(), P(("col", "row"), None))
    return jax.shard_map(
        per_device, mesh=mesh, in_specs=in_specs, out_specs=out_specs, check_vma=False
    )
```

```python
import functools
import math

import jax
import jax.numpy as jnp
from jax import lax
from jax.experimental import pallas as pl
from jax.experimental.pallas import tpu as pltpu
from jax.sharding import PartitionSpec as P

GROUP = 64
UNROLL = 64


def accumulate_kernel(backward, dest_ref, source_ref, count_ref, tiles_ref, panel_ref, out_ref):
    step = pl.program_id(0)
    group = tiles_ref.shape[0]
    out_blocks = out_ref.shape[0]
    in_blocks = panel_ref.shape[0]

    @pl.when(step == 0)
    def _():
        out_ref[...] = jnp.zeros_like(out_ref)

    base = step * group
    live_count = count_ref[0]

    def one_tile(i, checked):
        slot = base + i
        tile = tiles_ref[i]
        if checked:
            tile = jnp.where(slot < live_count, tile, jnp.zeros_like(tile))
        if backward:
            fetch = jnp.clip(dest_ref[slot], 0, in_blocks - 1)
            target = jnp.clip(source_ref[slot], 0, out_blocks - 1)
            contrib = lax.dot_general(
                tile, panel_ref[fetch], (((0,), (0,)), ((), ())),
                preferred_element_type=jnp.float32,
            )
        else:
            fetch = jnp.clip(source_ref[slot], 0, in_blocks - 1)
            target = jnp.clip(dest_ref[slot], 0, out_blocks - 1)
            contrib = jnp.dot(tile, panel_ref[fetch], preferred_element_type=jnp.float32)
        out_ref[target] += contrib

    @pl.when(base + group <= live_count)
    def _():
        @pl.loop(0, group, unroll=UNROLL)
        def _(i):
            one_tile(i, False)

    @pl.when((base < live_count) & (base + group > live_count))
    def _():
        @pl.loop(0, group, unroll=UNROLL)
        def _(i):
            one_tile(i, True)


def accumulate(tiles, dest_ids, source_ids, live_count, source_blocks, out_blocks, backward):
    slots, block, _ = tiles.shape
    width = source_blocks.shape[-1]
    in_blocks = source_blocks.shape[0]
    group = math.gcd(slots, GROUP)
    steps = slots // group

    def tile_map(g, dest, source, count):
        last = jnp.maximum(count[0] - 1, 0) // group
        return (jnp.minimum(g, last), 0, 0)

    flops = 2 * slots * block * block * width
    bytes_accessed = tiles.size * 2 + source_blocks.size * 2 + out_blocks * block * width * 4
    return pl.pallas_call(
        functools.partial(accumulate_kernel, backward),
        out_shape=jax.ShapeDtypeStruct((out_blocks, block, width), jnp.float32),
        grid_spec=pltpu.PrefetchScalarGridSpec(
            num_scalar_prefetch=3,
            grid=(steps,),
            in_specs=[
                pl.BlockSpec((group, block, block), tile_map),
                pl.BlockSpec((in_blocks, block, width), lambda g, d, s, c: (0, 0, 0)),
            ],
            out_specs=pl.BlockSpec((out_blocks, block, width), lambda g, d, s, c: (0, 0, 0)),
        ),
        compiler_params=pltpu.CompilerParams(
            dimension_semantics=("arbitrary",), vmem_limit_bytes=60 * 1024 * 1024
        ),
        cost_estimate=pl.CostEstimate(
            flops=flops, transcendentals=0, bytes_accessed=bytes_accessed
        ),
    )(dest_ids, source_ids, live_count.reshape(1), tiles, source_blocks)


def butterfly_kernel(steps, value_ref, out_ref, outgoing, narrow_slots, wide_slots,
                     send_sems, recv_sems):
    barrier = pltpu.get_barrier_semaphore()
    partners = []
    for axis, distance, narrow in steps:
        me = lax.axis_index(axis)
        bit = (me // distance) % 2
        partners.append((axis, me + distance - 2 * distance * bit, narrow))
    for axis, partner, narrow in partners:
        pl.semaphore_signal(
            barrier, 1, device_id={axis: partner}, device_id_type=pl.DeviceIdType.MESH
        )
    pl.semaphore_wait(barrier, len(partners))
    out_ref[...] = value_ref[...]
    narrow_index = 0
    wide_index = 0
    for index, (axis, partner, narrow) in enumerate(partners):
        if narrow:
            outgoing[...] = out_ref[...].astype(outgoing.dtype)
            source = outgoing
            landing = narrow_slots.at[narrow_index]
        else:
            source = out_ref
            landing = wide_slots.at[wide_index]
        copy = pltpu.make_async_remote_copy(
            src_ref=source,
            dst_ref=landing,
            send_sem=send_sems.at[index],
            recv_sem=recv_sems.at[index],
            device_id={axis: partner},
            device_id_type=pl.DeviceIdType.MESH,
        )
        copy.start()
        copy.wait_send()
        copy.wait_recv()
        if narrow:
            out_ref[...] = outgoing[...].astype(jnp.float32) + landing[...].astype(jnp.float32)
            narrow_index += 1
        else:
            out_ref[...] = out_ref[...] + landing[...]
            wide_index += 1


def butterfly_sum(value, axes, tag):
    steps = []
    for axis, size, narrow in axes:
        distance = 1
        while distance < size:
            steps.append((axis, distance, narrow))
            distance *= 2
    count = len(steps)
    narrow_count = max(sum(1 for step in steps if step[2]), 1)
    wide_count = max(count - narrow_count, 1)
    return pl.pallas_call(
        functools.partial(butterfly_kernel, tuple(steps)),
        out_shape=jax.ShapeDtypeStruct(value.shape, value.dtype),
        in_specs=[pl.BlockSpec(memory_space=pltpu.VMEM)],
        out_specs=pl.BlockSpec(memory_space=pltpu.VMEM),
        scratch_shapes=[
            pltpu.VMEM(value.shape, jnp.bfloat16),
            pltpu.VMEM((narrow_count,) + value.shape, jnp.bfloat16),
            pltpu.VMEM((wide_count,) + value.shape, value.dtype),
            pltpu.SemaphoreType.DMA((count,)),
            pltpu.SemaphoreType.DMA((count,)),
        ],
        compiler_params=pltpu.CompilerParams(collective_id=tag, has_side_effects=True),
    )(value)


def exchange_kernel(axis, size, spread, parts_ref, out_ref, local_sem, send_sems, recv_sems):
    me = lax.axis_index(axis)
    barrier = pltpu.get_barrier_semaphore()
    for shift in range(1, size):
        pl.semaphore_signal(
            barrier, 1, device_id={axis: lax.rem(me + shift, size)},
            device_id_type=pl.DeviceIdType.MESH,
        )
    pl.semaphore_wait(barrier, size - 1)
    copies = []
    for shift in range(1, size):
        peer = lax.rem(me + shift, size)
        copy = pltpu.make_async_remote_copy(
            src_ref=parts_ref if spread else parts_ref.at[peer],
            dst_ref=out_ref.at[me],
            send_sem=send_sems.at[shift],
            recv_sem=recv_sems.at[shift],
            device_id={axis: peer},
            device_id_type=pl.DeviceIdType.MESH,
        )
        copy.start()
        copies.append(copy)
    local = pltpu.make_async_copy(
        parts_ref if spread else parts_ref.at[me], out_ref.at[me], local_sem
    )
    local.start()
    local.wait()
    for copy in copies:
        copy.wait_send()
        copy.wait_recv()


def exchange(parts, axis, size, spread, tag):
    shape = (size,) + parts.shape[1 - spread:]
    nbytes = math.prod(shape) * parts.dtype.itemsize
    return pl.pallas_call(
        functools.partial(exchange_kernel, axis, size, spread),
        out_shape=jax.ShapeDtypeStruct(shape, parts.dtype),
        in_specs=[pl.BlockSpec(memory_space=pl.ANY)],
        out_specs=pl.BlockSpec(memory_space=pl.ANY),
        scratch_shapes=[
            pltpu.SemaphoreType.DMA,
            pltpu.SemaphoreType.DMA((size,)),
            pltpu.SemaphoreType.DMA((size,)),
        ],
        compiler_params=pltpu.CompilerParams(collective_id=tag, has_side_effects=True),
        cost_estimate=pl.CostEstimate(flops=0, transcendentals=0, bytes_accessed=2 * nbytes),
    )(parts)


def gather_all(value, axis, size):
    spread = jnp.broadcast_to(value[None], (size,) + value.shape)
    got = lax.all_to_all(spread, axis, 0, 0, tiled=False)
    return got.reshape((size * value.shape[0],) + value.shape[1:])


def scatter_sum_pallas(value, axis, size, tag):
    parts = value.reshape((size, value.shape[0] // size) + value.shape[1:])
    got = exchange(parts, axis, size, False, tag)
    return jnp.sum(got.astype(jnp.float32), axis=0)


def scatter_sum(value, axis, size):
    parts = value.reshape((size, value.shape[0] // size) + value.shape[1:])
    got = lax.all_to_all(parts, axis, 0, 0, tiled=False)
    return jnp.sum(got.astype(jnp.float32), axis=0)


def per_device(features, weight, bias, cotangent, tiles, tile_rows, tile_cols, tile_counts):
    tile_set = tiles[0, 0]
    dest_ids = tile_rows[0, 0]
    source_ids = tile_cols[0, 0]
    live_count = tile_counts[0, 0]
    block = tile_set.shape[-1]
    own_nodes = features.shape[0]
    width = features.shape[1]
    row_count = lax.axis_size("row")
    col_count = lax.axis_size("col")
    blocks_down = own_nodes * col_count // block
    blocks_across = own_nodes * row_count // block
    factor = 1.0 / math.sqrt(own_nodes * row_count * col_count)
    panel = gather_all(features, "row", row_count)
    panel_blocks = panel.reshape(blocks_across, block, width)
    partial_value = accumulate(
        tile_set, dest_ids, source_ids, live_count, panel_blocks, blocks_down, False
    )
    term = partial_value.reshape(blocks_down * block, width)
    summed = scatter_sum(term.astype(jnp.bfloat16), "col", col_count)
    aggregated = summed.astype(jnp.bfloat16)
    preact = jnp.dot(aggregated, weight, preferred_element_type=jnp.float32) + bias
    hidden = jax.nn.silu(preact).astype(jnp.bfloat16)
    sigma = jax.nn.sigmoid(preact)
    slope = sigma * (1.0 + preact * (1.0 - sigma))
    grad_pre = (cotangent.astype(jnp.float32) * slope).astype(jnp.bfloat16)
    local_weight = jnp.einsum("nf,ng->fg", aggregated, grad_pre, preferred_element_type=jnp.float32)
    local_bias = jnp.sum(grad_pre.astype(jnp.float32), axis=0)
    grad_agg = jnp.dot(grad_pre, weight.T, preferred_element_type=jnp.float32).astype(jnp.bfloat16)
    packed = jnp.concatenate([local_weight, local_bias[None, :]], axis=0)
    grad_panel = lax.all_gather(grad_agg, "col", axis=0, tiled=True)
    packed = butterfly_sum(packed, (("col", col_count, True), ("row", row_count, False)), 1)
    grad_panel, packed = lax.optimization_barrier((grad_panel, packed))
    grad_blocks = grad_panel.reshape(blocks_down, block, width)
    partial_back = accumulate(
        tile_set, dest_ids, source_ids, live_count, grad_blocks, blocks_across, True
    )
    term_back = partial_back.reshape(blocks_across * block, width)
    grad_features = scatter_sum_pallas(term_back.astype(jnp.bfloat16), "row", row_count, 0).astype(
        jnp.bfloat16
    )
    grad_weight = packed[:width] * factor
    grad_bias = packed[width] * factor
    return (hidden, grad_weight, grad_bias, grad_features)


def solution(mesh):
    in_specs = (
        P(("col", "row"), None),
        P(),
        P(),
        P(("row", "col"), None),
        P("row", "col", None, None, None),
        P("row", "col", None),
        P("row", "col", None),
        P("row", "col"),
    )
    out_specs = (P(("row", "col"), None), P(), P(), P(("col", "row"), None))
    return jax.shard_map(
        per_device, mesh=mesh, in_specs=in_specs, out_specs=out_specs, check_vma=False
    )
```

```python
import functools
import math

import jax
import jax.numpy as jnp
from jax import lax
from jax.experimental import pallas as pl
from jax.experimental.pallas import tpu as pltpu
from jax.sharding import PartitionSpec as P

GROUP = 64
UNROLL = 64


def accumulate_kernel(backward, dest_ref, source_ref, count_ref, tiles_ref, panel_ref, result_ref,
                      out_ref):
    step = pl.program_id(0)
    group = tiles_ref.shape[0]
    out_blocks = out_ref.shape[0]
    in_blocks = panel_ref.shape[0]

    @pl.when(step == 0)
    def _():
        out_ref[...] = jnp.zeros_like(out_ref)

    base = step * group
    live_count = count_ref[0]

    def one_tile(i, checked):
        slot = base + i
        tile = tiles_ref[i]
        if checked:
            tile = jnp.where(slot < live_count, tile, jnp.zeros_like(tile))
        if backward:
            fetch = jnp.clip(dest_ref[slot], 0, in_blocks - 1)
            target = jnp.clip(source_ref[slot], 0, out_blocks - 1)
            contrib = lax.dot_general(
                tile, panel_ref[fetch], (((0,), (0,)), ((), ())),
                preferred_element_type=jnp.float32,
            )
        else:
            fetch = jnp.clip(source_ref[slot], 0, in_blocks - 1)
            target = jnp.clip(dest_ref[slot], 0, out_blocks - 1)
            contrib = jnp.dot(tile, panel_ref[fetch], preferred_element_type=jnp.float32)
        out_ref[target] += contrib

    @pl.when(base + group <= live_count)
    def _():
        @pl.loop(0, group, unroll=UNROLL)
        def _(i):
            one_tile(i, False)

    @pl.when((base < live_count) & (base + group > live_count))
    def _():
        @pl.loop(0, group, unroll=UNROLL)
        def _(i):
            one_tile(i, True)

    @pl.when(step == pl.num_programs(0) - 1)
    def _():
        result_ref[...] = out_ref[...].astype(result_ref.dtype)


def accumulate(tiles, dest_ids, source_ids, live_count, source_blocks, out_blocks, backward):
    slots, block, _ = tiles.shape
    width = source_blocks.shape[-1]
    in_blocks = source_blocks.shape[0]
    group = math.gcd(slots, GROUP)
    steps = slots // group

    def tile_map(g, dest, source, count):
        last = jnp.maximum(count[0] - 1, 0) // group
        return (jnp.minimum(g, last), 0, 0)

    flops = 2 * slots * block * block * width
    bytes_accessed = tiles.size * 2 + source_blocks.size * 2 + out_blocks * block * width * 4
    return pl.pallas_call(
        functools.partial(accumulate_kernel, backward),
        out_shape=jax.ShapeDtypeStruct((out_blocks, block, width), jnp.bfloat16),
        grid_spec=pltpu.PrefetchScalarGridSpec(
            num_scalar_prefetch=3,
            grid=(steps,),
            in_specs=[
                pl.BlockSpec((group, block, block), tile_map),
                pl.BlockSpec((in_blocks, block, width), lambda g, d, s, c: (0, 0, 0)),
            ],
            out_specs=pl.BlockSpec((out_blocks, block, width), lambda g, d, s, c: (0, 0, 0)),
            scratch_shapes=[pltpu.VMEM((out_blocks, block, width), jnp.float32)],
        ),
        compiler_params=pltpu.CompilerParams(
            dimension_semantics=("arbitrary",), vmem_limit_bytes=60 * 1024 * 1024
        ),
        cost_estimate=pl.CostEstimate(
            flops=flops, transcendentals=0, bytes_accessed=bytes_accessed
        ),
    )(dest_ids, source_ids, live_count.reshape(1), tiles, source_blocks)


def butterfly_kernel(steps, value_ref, out_ref, outgoing, slots, send_sems, recv_sems):
    partners = []
    for axis, distance in steps:
        me = lax.axis_index(axis)
        bit = (me // distance) % 2
        partners.append((axis, me + distance - 2 * distance * bit))
    barrier = pltpu.get_barrier_semaphore()
    for axis, partner in partners:
        pl.semaphore_signal(
            barrier, 1, device_id={axis: partner}, device_id_type=pl.DeviceIdType.MESH
        )
    pl.semaphore_wait(barrier, len(partners))
    out_ref[...] = value_ref[...]
    for index, (axis, partner) in enumerate(partners):
        outgoing[...] = out_ref[...].astype(outgoing.dtype)
        copy = pltpu.make_async_remote_copy(
            src_ref=outgoing,
            dst_ref=slots.at[index],
            send_sem=send_sems.at[index],
            recv_sem=recv_sems.at[index],
            device_id={axis: partner},
            device_id_type=pl.DeviceIdType.MESH,
        )
        copy.start()
        copy.wait_send()
        copy.wait_recv()
        out_ref[...] = outgoing[...].astype(jnp.float32) + slots[index].astype(jnp.float32)


def butterfly_sum(value, axes, tag):
    steps = []
    for axis, size in axes:
        distance = 1
        while distance < size:
            steps.append((axis, distance))
            distance *= 2
    count = len(steps)
    return pl.pallas_call(
        functools.partial(butterfly_kernel, tuple(steps)),
        out_shape=jax.ShapeDtypeStruct(value.shape, value.dtype),
        in_specs=[pl.BlockSpec(memory_space=pltpu.VMEM)],
        out_specs=pl.BlockSpec(memory_space=pltpu.VMEM),
        scratch_shapes=[
            pltpu.VMEM(value.shape, jnp.bfloat16),
            pltpu.VMEM((count,) + value.shape, jnp.bfloat16),
            pltpu.SemaphoreType.DMA((count,)),
            pltpu.SemaphoreType.DMA((count,)),
        ],
        compiler_params=pltpu.CompilerParams(collective_id=tag, has_side_effects=True),
    )(value)


def gather_all(value, axis, size):
    spread = jnp.broadcast_to(value[None], (size,) + value.shape)
    got = lax.all_to_all(spread, axis, 0, 0, tiled=False)
    return got.reshape((size * value.shape[0],) + value.shape[1:])


def scatter_sum(value, axis, size):
    parts = value.reshape((size, value.shape[0] // size) + value.shape[1:])
    got = lax.all_to_all(parts, axis, 0, 0, tiled=False)
    return jnp.sum(got.astype(jnp.float32), axis=0)


def per_device(features, weight, bias, cotangent, tiles, tile_rows, tile_cols, tile_counts):
    tile_set = tiles[0, 0]
    dest_ids = tile_rows[0, 0]
    source_ids = tile_cols[0, 0]
    live_count = tile_counts[0, 0]
    block = tile_set.shape[-1]
    own_nodes = features.shape[0]
    width = features.shape[1]
    row_count = lax.axis_size("row")
    col_count = lax.axis_size("col")
    blocks_down = own_nodes * col_count // block
    blocks_across = own_nodes * row_count // block
    factor = 1.0 / math.sqrt(own_nodes * row_count * col_count)
    panel = gather_all(features, "row", row_count)
    panel_blocks = panel.reshape(blocks_across, block, width)
    partial_value = accumulate(
        tile_set, dest_ids, source_ids, live_count, panel_blocks, blocks_down, False
    )
    term = partial_value.reshape(blocks_down * block, width)
    summed = scatter_sum(term.astype(jnp.bfloat16), "col", col_count)
    aggregated = summed.astype(jnp.bfloat16)
    preact = jnp.dot(aggregated, weight, preferred_element_type=jnp.float32) + bias
    hidden = jax.nn.silu(preact).astype(jnp.bfloat16)
    sigma = jax.nn.sigmoid(preact)
    slope = sigma * (1.0 + preact * (1.0 - sigma))
    grad_pre = (cotangent.astype(jnp.float32) * slope).astype(jnp.bfloat16)
    local_weight = jnp.einsum("nf,ng->fg", aggregated, grad_pre, preferred_element_type=jnp.float32)
    local_bias = jnp.sum(grad_pre.astype(jnp.float32), axis=0)
    grad_agg = jnp.dot(grad_pre, weight.T, preferred_element_type=jnp.float32).astype(jnp.bfloat16)
    packed = jnp.concatenate([local_weight, local_bias[None, :]], axis=0)
    grad_panel = lax.all_gather(grad_agg, "col", axis=0, tiled=True)
    packed = butterfly_sum(packed, (("col", col_count), ("row", row_count)), 1)
    grad_panel, packed = lax.optimization_barrier((grad_panel, packed))
    grad_blocks = grad_panel.reshape(blocks_down, block, width)
    partial_back = accumulate(
        tile_set, dest_ids, source_ids, live_count, grad_blocks, blocks_across, True
    )
    term_back = partial_back.reshape(blocks_across * block, width)
    grad_features = scatter_sum(term_back.astype(jnp.bfloat16), "row", row_count).astype(
        jnp.bfloat16
    )
    grad_weight = packed[:width] * factor
    grad_bias = packed[width] * factor
    return (hidden, grad_weight, grad_bias, grad_features)


def solution(mesh):
    in_specs = (
        P(("col", "row"), None),
        P(),
        P(),
        P(("row", "col"), None),
        P("row", "col", None, None, None),
        P("row", "col", None),
        P("row", "col", None),
        P("row", "col"),
    )
    out_specs = (P(("row", "col"), None), P(), P(), P(("col", "row"), None))
    return jax.shard_map(
        per_device, mesh=mesh, in_specs=in_specs, out_specs=out_specs, check_vma=False
    )
```

```python
import functools
import math

import jax
import jax.numpy as jnp
from jax import lax
from jax.experimental import pallas as pl
from jax.experimental.pallas import tpu as pltpu
from jax.sharding import PartitionSpec as P

GROUP = 64
UNROLL = 64


def accumulate_kernel(backward, dest_ref, source_ref, count_ref, tiles_ref, panel_ref, result_ref,
                      out_ref):
    step = pl.program_id(0)
    group = tiles_ref.shape[0]
    out_blocks = out_ref.shape[0]
    in_blocks = panel_ref.shape[0]

    @pl.when(step == 0)
    def _():
        out_ref[...] = jnp.zeros_like(out_ref)

    base = step * group
    live_count = count_ref[0]

    def one_tile(i, checked):
        slot = base + i
        tile = tiles_ref[i]
        if checked:
            tile = jnp.where(slot < live_count, tile, jnp.zeros_like(tile))
        if backward:
            fetch = jnp.clip(dest_ref[slot], 0, in_blocks - 1)
            target = jnp.clip(source_ref[slot], 0, out_blocks - 1)
            contrib = lax.dot_general(
                tile, panel_ref[fetch], (((0,), (0,)), ((), ())),
                preferred_element_type=jnp.float32,
            )
        else:
            fetch = jnp.clip(source_ref[slot], 0, in_blocks - 1)
            target = jnp.clip(dest_ref[slot], 0, out_blocks - 1)
            contrib = jnp.dot(tile, panel_ref[fetch], preferred_element_type=jnp.float32)
        out_ref[target] += contrib

    @pl.when(base + group <= live_count)
    def _():
        @pl.loop(0, group, unroll=UNROLL)
        def _(i):
            one_tile(i, False)

    @pl.when((base < live_count) & (base + group > live_count))
    def _():
        @pl.loop(0, group, unroll=UNROLL)
        def _(i):
            one_tile(i, True)

    @pl.when(step == pl.num_programs(0) - 1)
    def _():
        result_ref[...] = out_ref[...].astype(result_ref.dtype)


def accumulate(tiles, dest_ids, source_ids, live_count, source_blocks, out_blocks, backward,
               out_dtype=jnp.bfloat16):
    slots, block, _ = tiles.shape
    width = source_blocks.shape[-1]
    in_blocks = source_blocks.shape[0]
    group = math.gcd(slots, GROUP)
    steps = slots // group

    def tile_map(g, dest, source, count):
        last = jnp.maximum(count[0] - 1, 0) // group
        return (jnp.minimum(g, last), 0, 0)

    flops = 2 * slots * block * block * width
    bytes_accessed = tiles.size * 2 + source_blocks.size * 2 + out_blocks * block * width * 4
    return pl.pallas_call(
        functools.partial(accumulate_kernel, backward),
        out_shape=jax.ShapeDtypeStruct((out_blocks, block, width), out_dtype),
        grid_spec=pltpu.PrefetchScalarGridSpec(
            num_scalar_prefetch=3,
            grid=(steps,),
            in_specs=[
                pl.BlockSpec((group, block, block), tile_map),
                pl.BlockSpec((in_blocks, block, width), lambda g, d, s, c: (0, 0, 0)),
            ],
            out_specs=pl.BlockSpec((out_blocks, block, width), lambda g, d, s, c: (0, 0, 0)),
            scratch_shapes=[pltpu.VMEM((out_blocks, block, width), jnp.float32)],
        ),
        compiler_params=pltpu.CompilerParams(
            dimension_semantics=("arbitrary",), vmem_limit_bytes=60 * 1024 * 1024
        ),
        cost_estimate=pl.CostEstimate(
            flops=flops, transcendentals=0, bytes_accessed=bytes_accessed
        ),
    )(dest_ids, source_ids, live_count.reshape(1), tiles, source_blocks)


def butterfly_kernel(steps, value_ref, out_ref, outgoing, slots, send_sems, recv_sems):
    partners = []
    for axis, distance in steps:
        me = lax.axis_index(axis)
        bit = (me // distance) % 2
        partners.append((axis, me + distance - 2 * distance * bit))
    barrier = pltpu.get_barrier_semaphore()
    for axis, partner in partners:
        pl.semaphore_signal(
            barrier, 1, device_id={axis: partner}, device_id_type=pl.DeviceIdType.MESH
        )
    pl.semaphore_wait(barrier, len(partners))
    out_ref[...] = value_ref[...]
    for index, (axis, partner) in enumerate(partners):
        outgoing[...] = out_ref[...].astype(outgoing.dtype)
        copy = pltpu.make_async_remote_copy(
            src_ref=outgoing,
            dst_ref=slots.at[index],
            send_sem=send_sems.at[index],
            recv_sem=recv_sems.at[index],
            device_id={axis: partner},
            device_id_type=pl.DeviceIdType.MESH,
        )
        copy.start()
        copy.wait_send()
        copy.wait_recv()
        out_ref[...] = outgoing[...].astype(jnp.float32) + slots[index].astype(jnp.float32)


def butterfly_sum(value, axes, tag):
    steps = []
    for axis, size in axes:
        distance = 1
        while distance < size:
            steps.append((axis, distance))
            distance *= 2
    count = len(steps)
    return pl.pallas_call(
        functools.partial(butterfly_kernel, tuple(steps)),
        out_shape=jax.ShapeDtypeStruct(value.shape, value.dtype),
        in_specs=[pl.BlockSpec(memory_space=pltpu.VMEM)],
        out_specs=pl.BlockSpec(memory_space=pltpu.VMEM),
        scratch_shapes=[
            pltpu.VMEM(value.shape, jnp.bfloat16),
            pltpu.VMEM((count,) + value.shape, jnp.bfloat16),
            pltpu.SemaphoreType.DMA((count,)),
            pltpu.SemaphoreType.DMA((count,)),
        ],
        compiler_params=pltpu.CompilerParams(collective_id=tag, has_side_effects=True),
    )(value)


def gather_all(value, axis, size):
    spread = jnp.broadcast_to(value[None], (size,) + value.shape)
    got = lax.all_to_all(spread, axis, 0, 0, tiled=False)
    return got.reshape((size * value.shape[0],) + value.shape[1:])


def scatter_sum(value, axis, size):
    parts = value.reshape((size, value.shape[0] // size) + value.shape[1:])
    got = lax.all_to_all(parts, axis, 0, 0, tiled=False)
    return jnp.sum(got.astype(jnp.float32), axis=0)


def scatter_sum_paired(value, axis, size):
    parity = lax.axis_index(axis) % 2
    chunks = value.reshape((size // 2, 2, value.shape[0] // size) + value.shape[1:])
    keep = jnp.where(parity == 0, chunks[:, 0], chunks[:, 1])
    send = jnp.where(parity == 0, chunks[:, 1], chunks[:, 0])
    got = lax.ppermute(send, axis, [(i, i ^ 1) for i in range(size)])
    paired = (keep + got).astype(jnp.bfloat16)
    groups = [list(range(start, size, 2)) for start in range(2)]
    spread = lax.all_to_all(paired, axis, 0, 0, tiled=False, axis_index_groups=groups)
    return jnp.sum(spread.astype(jnp.float32), axis=0)


def per_device(features, weight, bias, cotangent, tiles, tile_rows, tile_cols, tile_counts):
    tile_set = tiles[0, 0]
    dest_ids = tile_rows[0, 0]
    source_ids = tile_cols[0, 0]
    live_count = tile_counts[0, 0]
    block = tile_set.shape[-1]
    own_nodes = features.shape[0]
    width = features.shape[1]
    row_count = lax.axis_size("row")
    col_count = lax.axis_size("col")
    blocks_down = own_nodes * col_count // block
    blocks_across = own_nodes * row_count // block
    factor = 1.0 / math.sqrt(own_nodes * row_count * col_count)
    panel = gather_all(features, "row", row_count)
    panel_blocks = panel.reshape(blocks_across, block, width)
    partial_value = accumulate(
        tile_set, dest_ids, source_ids, live_count, panel_blocks, blocks_down, False, jnp.float32
    )
    term = partial_value.reshape(blocks_down * block, width)
    summed = scatter_sum_paired(term, "col", col_count)
    aggregated = summed.astype(jnp.bfloat16)
    preact = jnp.dot(aggregated, weight, preferred_element_type=jnp.float32) + bias
    hidden = jax.nn.silu(preact).astype(jnp.bfloat16)
    sigma = jax.nn.sigmoid(preact)
    slope = sigma * (1.0 + preact * (1.0 - sigma))
    grad_pre = (cotangent.astype(jnp.float32) * slope).astype(jnp.bfloat16)
    local_weight = jnp.einsum("nf,ng->fg", aggregated, grad_pre, preferred_element_type=jnp.float32)
    local_bias = jnp.sum(grad_pre.astype(jnp.float32), axis=0)
    grad_agg = jnp.dot(grad_pre, weight.T, preferred_element_type=jnp.float32).astype(jnp.bfloat16)
    packed = jnp.concatenate([local_weight, local_bias[None, :]], axis=0)
    grad_panel = lax.all_gather(grad_agg, "col", axis=0, tiled=True)
    packed = butterfly_sum(packed, (("col", col_count), ("row", row_count)), 1)
    grad_panel, packed = lax.optimization_barrier((grad_panel, packed))
    grad_blocks = grad_panel.reshape(blocks_down, block, width)
    partial_back = accumulate(
        tile_set, dest_ids, source_ids, live_count, grad_blocks, blocks_across, True
    )
    term_back = partial_back.reshape(blocks_across * block, width)
    grad_features = scatter_sum(term_back.astype(jnp.bfloat16), "row", row_count).astype(
        jnp.bfloat16
    )
    grad_weight = packed[:width] * factor
    grad_bias = packed[width] * factor
    return (hidden, grad_weight, grad_bias, grad_features)


def solution(mesh):
    in_specs = (
        P(("col", "row"), None),
        P(),
        P(),
        P(("row", "col"), None),
        P("row", "col", None, None, None),
        P("row", "col", None),
        P("row", "col", None),
        P("row", "col"),
    )
    out_specs = (P(("row", "col"), None), P(), P(), P(("col", "row"), None))
    return jax.shard_map(
        per_device, mesh=mesh, in_specs=in_specs, out_specs=out_specs, check_vma=False
    )
```

```python
import functools
import math

import jax
import jax.numpy as jnp
from jax import lax
from jax.experimental import pallas as pl
from jax.experimental.pallas import tpu as pltpu
from jax.sharding import PartitionSpec as P

GROUP = 64
UNROLL = 64


def accumulate_kernel(backward, split, dest_ref, source_ref, count_ref, tiles_ref, panel_ref,
                      *refs):
    out_ref = refs[-1]
    step = pl.program_id(0)
    group = tiles_ref.shape[0]
    out_blocks = out_ref.shape[0]
    in_blocks = panel_ref.shape[0]

    @pl.when(step == 0)
    def _():
        out_ref[...] = jnp.zeros_like(out_ref)

    base = step * group
    live_count = count_ref[0]

    def one_tile(i, checked):
        slot = base + i
        tile = tiles_ref[i]
        if checked:
            tile = jnp.where(slot < live_count, tile, jnp.zeros_like(tile))
        if backward:
            fetch = jnp.clip(dest_ref[slot], 0, in_blocks - 1)
            target = jnp.clip(source_ref[slot], 0, out_blocks - 1)
            contrib = lax.dot_general(
                tile, panel_ref[fetch], (((0,), (0,)), ((), ())),
                preferred_element_type=jnp.float32,
            )
        else:
            fetch = jnp.clip(source_ref[slot], 0, in_blocks - 1)
            target = jnp.clip(dest_ref[slot], 0, out_blocks - 1)
            contrib = jnp.dot(tile, panel_ref[fetch], preferred_element_type=jnp.float32)
        out_ref[target] += contrib

    @pl.when(base + group <= live_count)
    def _():
        @pl.loop(0, group, unroll=UNROLL)
        def _(i):
            one_tile(i, False)

    @pl.when((base < live_count) & (base + group > live_count))
    def _():
        @pl.loop(0, group, unroll=UNROLL)
        def _(i):
            one_tile(i, True)

    @pl.when(step == pl.num_programs(0) - 1)
    def _():
        if split:
            keep_ref, send_ref = refs[0], refs[1]
            per = keep_ref.shape[1]
            parity = lax.axis_index(split) % 2
            for k in range(keep_ref.shape[0]):
                keep_ref[k] = out_ref[pl.ds((2 * k + parity) * per, per)]
                send_ref[k] = out_ref[pl.ds((2 * k + 1 - parity) * per, per)]
        else:
            refs[0][...] = out_ref[...].astype(refs[0].dtype)


def accumulate(tiles, dest_ids, source_ids, live_count, source_blocks, out_blocks, backward,
               out_dtype=jnp.bfloat16, split=None, split_size=1):
    slots, block, _ = tiles.shape
    width = source_blocks.shape[-1]
    in_blocks = source_blocks.shape[0]
    group = math.gcd(slots, GROUP)
    steps = slots // group

    def tile_map(g, dest, source, count):
        last = jnp.maximum(count[0] - 1, 0) // group
        return (jnp.minimum(g, last), 0, 0)

    if split:
        half = split_size // 2
        per = out_blocks // split_size
        part = jax.ShapeDtypeStruct((half, per, block, width), jnp.float32)
        out_shape = (part, part)
        out_specs = (
            pl.BlockSpec((half, per, block, width), lambda g, d, s, c: (0, 0, 0, 0)),
        ) * 2
    else:
        out_shape = jax.ShapeDtypeStruct((out_blocks, block, width), out_dtype)
        out_specs = pl.BlockSpec((out_blocks, block, width), lambda g, d, s, c: (0, 0, 0))
    flops = 2 * slots * block * block * width
    bytes_accessed = tiles.size * 2 + source_blocks.size * 2 + out_blocks * block * width * 4
    return pl.pallas_call(
        functools.partial(accumulate_kernel, backward, split),
        out_shape=out_shape,
        grid_spec=pltpu.PrefetchScalarGridSpec(
            num_scalar_prefetch=3,
            grid=(steps,),
            in_specs=[
                pl.BlockSpec((group, block, block), tile_map),
                pl.BlockSpec((in_blocks, block, width), lambda g, d, s, c: (0, 0, 0)),
            ],
            out_specs=out_specs,
            scratch_shapes=[pltpu.VMEM((out_blocks, block, width), jnp.float32)],
        ),
        compiler_params=pltpu.CompilerParams(
            dimension_semantics=("arbitrary",), vmem_limit_bytes=60 * 1024 * 1024
        ),
        cost_estimate=pl.CostEstimate(
            flops=flops, transcendentals=0, bytes_accessed=bytes_accessed
        ),
    )(dest_ids, source_ids, live_count.reshape(1), tiles, source_blocks)


def butterfly_kernel(steps, value_ref, out_ref, outgoing, slots, send_sems, recv_sems):
    partners = []
    for axis, distance in steps:
        me = lax.axis_index(axis)
        bit = (me // distance) % 2
        partners.append((axis, me + distance - 2 * distance * bit))
    barrier = pltpu.get_barrier_semaphore()
    for axis, partner in partners:
        pl.semaphore_signal(
            barrier, 1, device_id={axis: partner}, device_id_type=pl.DeviceIdType.MESH
        )
    pl.semaphore_wait(barrier, len(partners))
    out_ref[...] = value_ref[...]
    for index, (axis, partner) in enumerate(partners):
        outgoing[...] = out_ref[...].astype(outgoing.dtype)
        copy = pltpu.make_async_remote_copy(
            src_ref=outgoing,
            dst_ref=slots.at[index],
            send_sem=send_sems.at[index],
            recv_sem=recv_sems.at[index],
            device_id={axis: partner},
            device_id_type=pl.DeviceIdType.MESH,
        )
        copy.start()
        copy.wait_send()
        copy.wait_recv()
        out_ref[...] = outgoing[...].astype(jnp.float32) + slots[index].astype(jnp.float32)


def butterfly_sum(value, axes, tag):
    steps = []
    for axis, size in axes:
        distance = 1
        while distance < size:
            steps.append((axis, distance))
            distance *= 2
    count = len(steps)
    return pl.pallas_call(
        functools.partial(butterfly_kernel, tuple(steps)),
        out_shape=jax.ShapeDtypeStruct(value.shape, value.dtype),
        in_specs=[pl.BlockSpec(memory_space=pltpu.VMEM)],
        out_specs=pl.BlockSpec(memory_space=pltpu.VMEM),
        scratch_shapes=[
            pltpu.VMEM(value.shape, jnp.bfloat16),
            pltpu.VMEM((count,) + value.shape, jnp.bfloat16),
            pltpu.SemaphoreType.DMA((count,)),
            pltpu.SemaphoreType.DMA((count,)),
        ],
        compiler_params=pltpu.CompilerParams(collective_id=tag, has_side_effects=True),
    )(value)


def gather_all(value, axis, size):
    spread = jnp.broadcast_to(value[None], (size,) + value.shape)
    got = lax.all_to_all(spread, axis, 0, 0, tiled=False)
    return got.reshape((size * value.shape[0],) + value.shape[1:])


def scatter_sum(value, axis, size):
    parts = value.reshape((size, value.shape[0] // size) + value.shape[1:])
    got = lax.all_to_all(parts, axis, 0, 0, tiled=False)
    return jnp.sum(got.astype(jnp.float32), axis=0)


def scatter_sum_paired(keep, send, axis, size):
    got = lax.ppermute(send, axis, [(i, i ^ 1) for i in range(size)])
    paired = (keep + got).astype(jnp.bfloat16)
    groups = [list(range(start, size, 2)) for start in range(2)]
    spread = lax.all_to_all(paired, axis, 0, 0, tiled=False, axis_index_groups=groups)
    return jnp.sum(spread.astype(jnp.float32), axis=0)


def per_device(features, weight, bias, cotangent, tiles, tile_rows, tile_cols, tile_counts):
    tile_set = tiles[0, 0]
    dest_ids = tile_rows[0, 0]
    source_ids = tile_cols[0, 0]
    live_count = tile_counts[0, 0]
    block = tile_set.shape[-1]
    own_nodes = features.shape[0]
    width = features.shape[1]
    row_count = lax.axis_size("row")
    col_count = lax.axis_size("col")
    blocks_down = own_nodes * col_count // block
    blocks_across = own_nodes * row_count // block
    factor = 1.0 / math.sqrt(own_nodes * row_count * col_count)
    panel = gather_all(features, "row", row_count)
    panel_blocks = panel.reshape(blocks_across, block, width)
    keep, send = accumulate(
        tile_set, dest_ids, source_ids, live_count, panel_blocks, blocks_down, False,
        split="col", split_size=col_count,
    )
    chunk_shape = (col_count // 2, own_nodes, width)
    summed = scatter_sum_paired(
        keep.reshape(chunk_shape), send.reshape(chunk_shape), "col", col_count
    )
    aggregated = summed.astype(jnp.bfloat16)
    preact = jnp.dot(aggregated, weight, preferred_element_type=jnp.float32) + bias
    hidden = jax.nn.silu(preact).astype(jnp.bfloat16)
    sigma = jax.nn.sigmoid(preact)
    slope = sigma * (1.0 + preact * (1.0 - sigma))
    grad_pre = (cotangent.astype(jnp.float32) * slope).astype(jnp.bfloat16)
    local_weight = jnp.einsum("nf,ng->fg", aggregated, grad_pre, preferred_element_type=jnp.float32)
    local_bias = jnp.sum(grad_pre.astype(jnp.float32), axis=0)
    grad_agg = jnp.dot(grad_pre, weight.T, preferred_element_type=jnp.float32).astype(jnp.bfloat16)
    packed = jnp.concatenate([local_weight, local_bias[None, :]], axis=0)
    grad_panel = lax.all_gather(grad_agg, "col", axis=0, tiled=True)
    packed = butterfly_sum(packed, (("col", col_count), ("row", row_count)), 1)
    grad_panel, packed = lax.optimization_barrier((grad_panel, packed))
    grad_blocks = grad_panel.reshape(blocks_down, block, width)
    partial_back = accumulate(
        tile_set, dest_ids, source_ids, live_count, grad_blocks, blocks_across, True
    )
    term_back = partial_back.reshape(blocks_across * block, width)
    grad_features = scatter_sum(term_back.astype(jnp.bfloat16), "row", row_count).astype(
        jnp.bfloat16
    )
    grad_weight = packed[:width] * factor
    grad_bias = packed[width] * factor
    return (hidden, grad_weight, grad_bias, grad_features)


def solution(mesh):
    in_specs = (
        P(("col", "row"), None),
        P(),
        P(),
        P(("row", "col"), None),
        P("row", "col", None, None, None),
        P("row", "col", None),
        P("row", "col", None),
        P("row", "col"),
    )
    out_specs = (P(("row", "col"), None), P(), P(), P(("col", "row"), None))
    return jax.shard_map(
        per_device, mesh=mesh, in_specs=in_specs, out_specs=out_specs, check_vma=False
    )
```

```python
import functools
import math

import jax
import jax.numpy as jnp
from jax import lax
from jax.experimental import pallas as pl
from jax.experimental.pallas import tpu as pltpu
from jax.sharding import PartitionSpec as P

GROUP = 128
UNROLL = 128


def accumulate_kernel(backward, split, dest_ref, source_ref, count_ref, tiles_ref, panel_ref,
                      *refs):
    out_ref = refs[-1]
    step = pl.program_id(0)
    group = tiles_ref.shape[0]
    out_blocks = out_ref.shape[0]
    in_blocks = panel_ref.shape[0]

    @pl.when(step == 0)
    def _():
        out_ref[...] = jnp.zeros_like(out_ref)

    base = step * group
    live_count = count_ref[0]

    def one_tile(i, checked):
        slot = base + i
        tile = tiles_ref[i]
        if checked:
            tile = jnp.where(slot < live_count, tile, jnp.zeros_like(tile))
        if backward:
            fetch = jnp.clip(dest_ref[slot], 0, in_blocks - 1)
            target = jnp.clip(source_ref[slot], 0, out_blocks - 1)
            contrib = lax.dot_general(
                tile, panel_ref[fetch], (((0,), (0,)), ((), ())),
                preferred_element_type=jnp.float32,
            )
        else:
            fetch = jnp.clip(source_ref[slot], 0, in_blocks - 1)
            target = jnp.clip(dest_ref[slot], 0, out_blocks - 1)
            contrib = jnp.dot(tile, panel_ref[fetch], preferred_element_type=jnp.float32)
        out_ref[target] += contrib

    @pl.when(base + group <= live_count)
    def _():
        @pl.loop(0, group, unroll=UNROLL)
        def _(i):
            one_tile(i, False)

    @pl.when((base < live_count) & (base + group > live_count))
    def _():
        @pl.loop(0, group, unroll=UNROLL)
        def _(i):
            one_tile(i, True)

    @pl.when(step == pl.num_programs(0) - 1)
    def _():
        if split:
            keep_ref, send_ref = refs[0], refs[1]
            per = keep_ref.shape[1]
            parity = lax.axis_index(split) % 2
            for k in range(keep_ref.shape[0]):
                keep_ref[k] = out_ref[pl.ds((2 * k + parity) * per, per)]
                send_ref[k] = out_ref[pl.ds((2 * k + 1 - parity) * per, per)]
        else:
            refs[0][...] = out_ref[...].astype(refs[0].dtype)


def accumulate(tiles, dest_ids, source_ids, live_count, source_blocks, out_blocks, backward,
               out_dtype=jnp.bfloat16, split=None, split_size=1):
    slots, block, _ = tiles.shape
    width = source_blocks.shape[-1]
    in_blocks = source_blocks.shape[0]
    group = math.gcd(slots, GROUP)
    steps = slots // group

    def tile_map(g, dest, source, count):
        last = jnp.maximum(count[0] - 1, 0) // group
        return (jnp.minimum(g, last), 0, 0)

    if split:
        half = split_size // 2
        per = out_blocks // split_size
        part = jax.ShapeDtypeStruct((half, per, block, width), jnp.float32)
        out_shape = (part, part)
        out_specs = (
            pl.BlockSpec((half, per, block, width), lambda g, d, s, c: (0, 0, 0, 0)),
        ) * 2
    else:
        out_shape = jax.ShapeDtypeStruct((out_blocks, block, width), out_dtype)
        out_specs = pl.BlockSpec((out_blocks, block, width), lambda g, d, s, c: (0, 0, 0))
    flops = 2 * slots * block * block * width
    bytes_accessed = tiles.size * 2 + source_blocks.size * 2 + out_blocks * block * width * 4
    return pl.pallas_call(
        functools.partial(accumulate_kernel, backward, split),
        out_shape=out_shape,
        grid_spec=pltpu.PrefetchScalarGridSpec(
            num_scalar_prefetch=3,
            grid=(steps,),
            in_specs=[
                pl.BlockSpec((group, block, block), tile_map),
                pl.BlockSpec((in_blocks, block, width), lambda g, d, s, c: (0, 0, 0)),
            ],
            out_specs=out_specs,
            scratch_shapes=[pltpu.VMEM((out_blocks, block, width), jnp.float32)],
        ),
        compiler_params=pltpu.CompilerParams(
            dimension_semantics=("arbitrary",), vmem_limit_bytes=60 * 1024 * 1024
        ),
        cost_estimate=pl.CostEstimate(
            flops=flops, transcendentals=0, bytes_accessed=bytes_accessed
        ),
    )(dest_ids, source_ids, live_count.reshape(1), tiles, source_blocks)


def butterfly_kernel(steps, value_ref, out_ref, outgoing, slots, send_sems, recv_sems):
    partners = []
    for axis, distance in steps:
        me = lax.axis_index(axis)
        bit = (me // distance) % 2
        partners.append((axis, me + distance - 2 * distance * bit))
    barrier = pltpu.get_barrier_semaphore()
    for axis, partner in partners:
        pl.semaphore_signal(
            barrier, 1, device_id={axis: partner}, device_id_type=pl.DeviceIdType.MESH
        )
    pl.semaphore_wait(barrier, len(partners))
    out_ref[...] = value_ref[...]
    for index, (axis, partner) in enumerate(partners):
        outgoing[...] = out_ref[...].astype(outgoing.dtype)
        copy = pltpu.make_async_remote_copy(
            src_ref=outgoing,
            dst_ref=slots.at[index],
            send_sem=send_sems.at[index],
            recv_sem=recv_sems.at[index],
            device_id={axis: partner},
            device_id_type=pl.DeviceIdType.MESH,
        )
        copy.start()
        copy.wait_send()
        copy.wait_recv()
        out_ref[...] = outgoing[...].astype(jnp.float32) + slots[index].astype(jnp.float32)


def butterfly_sum(value, axes, tag):
    steps = []
    for axis, size in axes:
        distance = 1
        while distance < size:
            steps.append((axis, distance))
            distance *= 2
    count = len(steps)
    return pl.pallas_call(
        functools.partial(butterfly_kernel, tuple(steps)),
        out_shape=jax.ShapeDtypeStruct(value.shape, value.dtype),
        in_specs=[pl.BlockSpec(memory_space=pltpu.VMEM)],
        out_specs=pl.BlockSpec(memory_space=pltpu.VMEM),
        scratch_shapes=[
            pltpu.VMEM(value.shape, jnp.bfloat16),
            pltpu.VMEM((count,) + value.shape, jnp.bfloat16),
            pltpu.SemaphoreType.DMA((count,)),
            pltpu.SemaphoreType.DMA((count,)),
        ],
        compiler_params=pltpu.CompilerParams(collective_id=tag, has_side_effects=True),
    )(value)


def gather_all(value, axis, size):
    spread = jnp.broadcast_to(value[None], (size,) + value.shape)
    got = lax.all_to_all(spread, axis, 0, 0, tiled=False)
    return got.reshape((size * value.shape[0],) + value.shape[1:])


def scatter_sum(value, axis, size):
    parts = value.reshape((size, value.shape[0] // size) + value.shape[1:])
    got = lax.all_to_all(parts, axis, 0, 0, tiled=False)
    return jnp.sum(got.astype(jnp.float32), axis=0)


def scatter_sum_paired(keep, send, axis, size):
    got = lax.ppermute(send, axis, [(i, i ^ 1) for i in range(size)])
    paired = (keep + got).astype(jnp.bfloat16)
    groups = [list(range(start, size, 2)) for start in range(2)]
    spread = lax.all_to_all(paired, axis, 0, 0, tiled=False, axis_index_groups=groups)
    return jnp.sum(spread.astype(jnp.float32), axis=0)


def per_device(features, weight, bias, cotangent, tiles, tile_rows, tile_cols, tile_counts):
    tile_set = tiles[0, 0]
    dest_ids = tile_rows[0, 0]
    source_ids = tile_cols[0, 0]
    live_count = tile_counts[0, 0]
    block = tile_set.shape[-1]
    own_nodes = features.shape[0]
    width = features.shape[1]
    row_count = lax.axis_size("row")
    col_count = lax.axis_size("col")
    blocks_down = own_nodes * col_count // block
    blocks_across = own_nodes * row_count // block
    factor = 1.0 / math.sqrt(own_nodes * row_count * col_count)
    panel = gather_all(features, "row", row_count)
    panel_blocks = panel.reshape(blocks_across, block, width)
    keep, send = accumulate(
        tile_set, dest_ids, source_ids, live_count, panel_blocks, blocks_down, False,
        split="col", split_size=col_count,
    )
    chunk_shape = (col_count // 2, own_nodes, width)
    summed = scatter_sum_paired(
        keep.reshape(chunk_shape), send.reshape(chunk_shape), "col", col_count
    )
    aggregated = summed.astype(jnp.bfloat16)
    preact = jnp.dot(aggregated, weight, preferred_element_type=jnp.float32) + bias
    hidden = jax.nn.silu(preact).astype(jnp.bfloat16)
    sigma = jax.nn.sigmoid(preact)
    slope = sigma * (1.0 + preact * (1.0 - sigma))
    grad_pre = (cotangent.astype(jnp.float32) * slope).astype(jnp.bfloat16)
    local_weight = jnp.einsum("nf,ng->fg", aggregated, grad_pre, preferred_element_type=jnp.float32)
    local_bias = jnp.sum(grad_pre.astype(jnp.float32), axis=0)
    grad_agg = jnp.dot(grad_pre, weight.T, preferred_element_type=jnp.float32).astype(jnp.bfloat16)
    packed = jnp.concatenate([local_weight, local_bias[None, :]], axis=0)
    grad_panel = lax.all_gather(grad_agg, "col", axis=0, tiled=True)
    packed = butterfly_sum(packed, (("col", col_count), ("row", row_count)), 1)
    grad_panel, packed = lax.optimization_barrier((grad_panel, packed))
    grad_blocks = grad_panel.reshape(blocks_down, block, width)
    partial_back = accumulate(
        tile_set, dest_ids, source_ids, live_count, grad_blocks, blocks_across, True
    )
    term_back = partial_back.reshape(blocks_across * block, width)
    grad_features = scatter_sum(term_back.astype(jnp.bfloat16), "row", row_count).astype(
        jnp.bfloat16
    )
    grad_weight = packed[:width] * factor
    grad_bias = packed[width] * factor
    return (hidden, grad_weight, grad_bias, grad_features)


def solution(mesh):
    in_specs = (
        P(("col", "row"), None),
        P(),
        P(),
        P(("row", "col"), None),
        P("row", "col", None, None, None),
        P("row", "col", None),
        P("row", "col", None),
        P("row", "col"),
    )
    out_specs = (P(("row", "col"), None), P(), P(), P(("col", "row"), None))
    return jax.shard_map(
        per_device, mesh=mesh, in_specs=in_specs, out_specs=out_specs, check_vma=False
    )
```
